512 devices in a mesh: seq: 64 (over z, x, core), head: 8 (over y).
Axes of the slice: x: 4, y: 8, z: 8, core: 2. Of those that a mesh axis runs over, the one named last changes fastest.
Arguments:
- xbc: bfloat16 [24576, 10240], P('seq', 'head'), may hold values from -6 to 6
- gate_z: bfloat16 [24576, 8192], P('seq', 'head'), may hold values from -6 to 6
- dt_raw: bfloat16 [128, 24576], P('head', 'seq'), may hold values from -3 to 3
- dt_bias: float32 [128], P('head'), may hold values from -1 to 0.5
- a_log: float32 [128], P('head'), may hold values from -11.5 to -6.6
- skip_d: float32 [128], P('head'), may hold values from 0.5 to 1.5
- conv_weight: float32 [4, 10240], P(None, 'head'), may hold values from -3 to 3
- conv_bias: float32 [10240], P('head'), may hold values from -3 to 3
- norm_gain: float32 [8192], P('head'), may hold values from 0.1 to 1.9
- out_weight: bfloat16 [8192, 4096], P('head', 'seq'), may hold values from -0.1875 to 0.1875
- starts: int32 [24576], P('seq'), may hold values from 0 to 1, as said below
Outputs:
- mixed: bfloat16 [24576, 4096], P('seq', 'head')
The draws below stay inside these ranges and needn't reach their ends.
Inputs may be any that keep to these rules, and one draw needn't show every extreme that they name: `starts`: a 0 or 1 flag for every token; every 1 lies among the first 6144 tokens, and there is at least one.
All inputs are finite; a program needn't handle non-finite values.
Results may differ from the reference program's by a relative error of at most 0.013.
Values may be sent and summed in bfloat16 or wider, within the bound.
A program may use at most 128 MiB of HBM per device.

```python
import jax
import jax.numpy as jnp
from jax import lax

D = 4096
H = 128
P_SIZE = 64
N = 128
G = 8
CONV = 4
TOK_DEV = 384
TOKENS = 24576
DI = 8192
HG = 16
GW = 1280
N_HEAD = 8


def draw_starts(key, part):
    first_key = jax.random.fold_in(key, 11)
    place_key = jax.random.fold_in(key, 12)
    quarter = TOKENS // 4
    places = jnp.arange(TOKENS)
    rolls = jax.random.randint(first_key, (TOKENS,), 0, 4 * TOK_DEV)
    forced = jax.random.randint(place_key, (), 0, quarter)
    flags = (rolls == 0) & (places < quarter) | (places == forced)
    return flags.astype(jnp.int32)


def strengthened(array, stream_key, source, target, blocks, factor):
    def block_of(axis_at):
        return (jnp.arange(array.shape[axis_at]) // (array.shape[axis_at] // blocks)).reshape((-1,) + (1,) * (array.ndim - 1 - axis_at))

    near = jax.random.permutation(stream_key, blocks)[block_of(target)]
    far = (block_of(target) + blocks // 2) % blocks
    return jnp.where((block_of(source) == near) | (block_of(source) == far), factor * array, array)


def block_scale(rng, extent, shards, least, largest):
    gain = 1.0
    for axis_at, blocks in shards:
        steps = jax.random.uniform(jax.random.fold_in(jax.random.fold_in(rng, 6), axis_at), (blocks,), jnp.float32, least / len(shards), largest / len(shards))
        gain = gain * jnp.repeat(jnp.exp(steps), extent[axis_at] // blocks).reshape((-1,) + (1,) * (len(extent) - 1 - axis_at))
    return gain


def noise(stream_key, dims, scale, most, split=(), kind=jnp.bfloat16):
    factor_of = block_scale(stream_key, dims, split, -0.22, 0.18) if split else 1.0
    values = jax.random.normal(stream_key, dims, jnp.float32) * scale * factor_of
    return jnp.minimum(jnp.maximum(values, -most), most).astype(kind)


def gaussian_with(own_key, extent, deviation, most, pieces, heavy, dtype=jnp.bfloat16):
    drawn = deviation * jax.random.normal(own_key, extent, jnp.float32)
    if pieces:
        drawn = drawn * block_scale(own_key, extent, pieces, -0.22, 0.18)
    return jnp.clip(strengthened(drawn, jax.random.fold_in(own_key, 3), *heavy), -most, most).astype(dtype)


def setup_inputs(seed: int = 0) -> dict:
    splits = jax.random.split(jax.random.key(seed), 12)
    xbc = noise(splits[0], (TOKENS, G * GW), 1.0, 6.0, ((0, 64), (1, 8)))
    gate_z = noise(splits[1], (TOKENS, DI), 1.0, 6.0, ((0, 64), (1, 8)))
    dt_raw = noise(splits[2], (H, TOKENS), 1.0, 3.0, ((0, 8), (1, 64)))
    dt_bias = jnp.clip(-1.0 + 1.5 * jax.random.uniform(splits[3], (H,), jnp.float32) ** block_scale(splits[3], (H,), ((0, 8),), -0.2, 0.2), -1.0, 0.5)
    a_log = jnp.clip(-11.5 + 4.9 * jax.random.uniform(splits[4], (H,), jnp.float32) ** block_scale(splits[4], (H,), ((0, 8),), -0.2, 0.2), -11.5, -6.6)
    skip_d = jnp.clip(0.5 + 1.0 * jax.random.uniform(splits[5], (H,), jnp.float32) ** block_scale(splits[5], (H,), ((0, 8),), -0.2, 0.2), 0.5, 1.5)
    conv_weight = noise(splits[6], (CONV, G * GW), CONV ** -0.5, 3.0, ((1, 8),), jnp.float32)
    conv_bias = noise(splits[7], (G * GW,), 0.5, 3.0, ((0, 8),), jnp.float32)
    norm_gain = jnp.clip(1.0 + 0.18 * jax.random.normal(splits[8], (DI,), jnp.float32), 0.1, 1.9)
    out_weight = gaussian_with(splits[9], (DI, D), DI ** -0.5, 0.1875, ((0, 8), (1, 64)), (0, 1, 64, 4.0))
    starts = draw_starts(jax.random.fold_in(splits[11], 71), 0)
    return {"xbc": xbc, "gate_z": gate_z, "dt_raw": dt_raw, "dt_bias": dt_bias, "a_log": a_log, "skip_d": skip_d, "conv_weight": conv_weight, "conv_bias": conv_bias, "norm_gain": norm_gain, "out_weight": out_weight, "starts": starts}


def conv_section(xbc, conv_weight, conv_bias, series):
    count = xbc.shape[0]
    width = conv_weight.shape[0]
    values = xbc.astype(jnp.float32)
    places = jnp.arange(count)
    acc = conv_bias[None, :] + conv_weight[width - 1][None, :] * values
    for lag in range(1, width):
        shifted = jnp.pad(values, ((lag, 0), (0, 0)))[:count]
        earlier = jnp.pad(series, (lag, 0))[:count]
        keep = ((series == earlier) & (places >= lag)).astype(jnp.float32)
        acc = acc + conv_weight[width - 1 - lag][None, :] * shifted * keep[:, None]
    return jax.nn.silu(acc).astype(jnp.bfloat16)

def to_half(value):
    return lax.optimization_barrier(value.astype(jnp.bfloat16)).astype(jnp.float32)

def reference(xbc, gate_z, dt_raw, dt_bias, a_log, skip_d, conv_weight, conv_bias, norm_gain, out_weight, starts):
    block_len = min(128, TOK_DEV)
    count = xbc.shape[0]
    series = jnp.cumsum(starts).astype(jnp.int32)
    unit = conv_section(xbc, conv_weight, conv_bias, series)
    grid = unit.reshape(count, G, GW).astype(jnp.float32)
    xs = grid[:, :, :HG * P_SIZE].reshape(count, H, P_SIZE)
    bmat = grid[:, :, HG * P_SIZE:HG * P_SIZE + N]
    cmat = grid[:, :, HG * P_SIZE + N:]
    steps_dt = jax.nn.softplus(dt_raw.astype(jnp.float32) + dt_bias[:, None])
    logs = -jnp.exp(a_log)[:, None] * steps_dt
    nblk = count // block_len
    xs_b = xs.reshape(nblk, block_len, H, P_SIZE)
    b_b = bmat.reshape(nblk, block_len, G, N)
    c_b = cmat.reshape(nblk, block_len, G, N)
    dt_b = steps_dt.reshape(H, nblk, block_len).transpose(1, 0, 2)
    log_b = logs.reshape(H, nblk, block_len).transpose(1, 0, 2)
    st_b = starts.reshape(nblk, block_len)
    lower = jnp.arange(block_len)[:, None] >= jnp.arange(block_len)[None, :]

    def step(state, inputs):
        xc, bc, cc, dtc, lc, sc = inputs
        cumul = jnp.cumsum(lc, axis=1)
        runs = jnp.cumsum(sc).astype(jnp.int32)
        same = lower & (runs[:, None] == runs[None, :])
        diff = cumul[:, :, None] - cumul[:, None, :]
        wdec = jnp.where(same[None], jnp.exp(jnp.minimum(diff, 0.0)), 0.0)
        scores = jnp.einsum('tgn,sgn->gts', cc, bc)
        scores_h = jnp.repeat(scores, HG, axis=0)
        weights = to_half(scores_h * wdec * dtc[:, None, :])
        y_diag = jnp.einsum('hts,shp->thp', weights, xc)
        enter = jnp.exp(cumul) * (runs == 0).astype(jnp.float32)[None, :]
        c_h = jnp.repeat(cc, HG, axis=1)
        b_h = jnp.repeat(bc, HG, axis=1)
        y_off = jnp.einsum('thn,hpn->thp', c_h, to_half(state)) * enter.T[:, :, None]
        tail = jnp.where((runs == runs[-1])[None, :], jnp.exp(jnp.minimum(cumul[:, -1:] - cumul, 0.0)), 0.0) * dtc
        bw = to_half(tail[:, :, None] * jnp.swapaxes(b_h, 0, 1))
        total = jnp.exp(cumul[:, -1]) * (runs[-1] == 0).astype(jnp.float32)
        new_state = state * total[:, None, None] + jnp.einsum('shp,hsn->hpn', xc, bw)
        y = y_diag + y_off + skip_d[None, :, None] * xc
        return (new_state, y)
    init = jnp.zeros((H, P_SIZE, N), jnp.float32)
    last, ys = lax.scan(step, init, (xs_b, b_b, c_b, dt_b, log_b, st_b))
    y = ys.reshape(count, H * P_SIZE)
    gated = y * jax.nn.silu(gate_z.astype(jnp.float32))
    mean_sq = lax.optimization_barrier(jnp.mean(gated * gated, axis=1))
    normed = (gated * lax.rsqrt(mean_sq + 1e-05)[:, None] * norm_gain[None, :]).astype(jnp.bfloat16)
    part = H * P_SIZE // N_HEAD
    acc = jnp.zeros((count, out_weight.shape[1]), jnp.float32)
    for index in range(N_HEAD):
        partial_value = jnp.dot(normed[:, index * part:(index + 1) * part], out_weight[index * part:(index + 1) * part], preferred_element_type=jnp.float32)
        acc = acc + partial_value.astype(jnp.bfloat16).astype(jnp.float32)
    return acc.astype(jnp.bfloat16)
```

```python
import jax
import jax.numpy as jnp
from jax import lax
from jax.experimental import pallas as pl
from jax.experimental.pallas import tpu as pltpu
from jax.sharding import PartitionSpec as P

P_SIZE = 64
N = 128
DI = 8192
HG = 16
GW = 1280


def passed_along(block, axis, distance):
    devices = range(lax.axis_size(axis))
    route = [(i - distance, i) for i in devices if i - distance in devices]
    return lax.ppermute(block, axis, route)


MESH = pl.DeviceIdType.MESH
ROW = 8


def decay_of(tile):
    both = tile.astype(jnp.float32)
    return both[0:1] + both[8:9]


def states_kernel(
    mine_ref, out_ref, row_buf, total_buf, column_buf, back_buf, land_buf, s1, r1, s2, r2, s3, r3
):
    place = lax.axis_index("seq")
    z = place // ROW
    j = place % ROW
    row_peers = [(j + k) % ROW for k in range(1, ROW)]
    column_peers = [(z + k) % ROW for k in range(1, ROW)]
    barrier = pltpu.get_barrier_semaphore()
    for peer in row_peers:
        pl.semaphore_signal(barrier, 1, device_id={"seq": z * ROW + peer}, device_id_type=MESH)
    for peer in column_peers:
        pl.semaphore_signal(barrier, 1, device_id={"seq": peer * ROW + j}, device_id_type=MESH)
    pl.semaphore_wait(barrier, 2 * (ROW - 1))
    copies = []
    for k, peer in enumerate(row_peers):
        copies.append(
            pltpu.make_async_remote_copy(
                mine_ref.at[peer], row_buf.at[j], s1.at[k], r1.at[k],
                device_id={"seq": z * ROW + peer}, device_id_type=MESH,
            )
        )
        copies[-1].start()
    row_buf[j] = mine_ref[j]
    for copy in copies:
        copy.wait()
    for head in range(2):
        total = row_buf[0, head, :P_SIZE].astype(jnp.float32)
        decay = decay_of(row_buf[0, head, P_SIZE:])
        for i in range(1, ROW):
            one = decay_of(row_buf[i, head, P_SIZE:])
            total = total * one + row_buf[i, head, :P_SIZE].astype(jnp.float32)
            decay = decay * one
        total_buf[head, :P_SIZE] = total.astype(jnp.bfloat16)
        high = decay.astype(jnp.bfloat16)
        low = decay - high.astype(jnp.float32)
        pair = jnp.concatenate(
            [jnp.broadcast_to(high.astype(jnp.float32), (8, N)), jnp.broadcast_to(low, (8, N))], axis=0
        )
        total_buf[head, P_SIZE:] = pair.astype(jnp.bfloat16)
    copies = []
    for k, peer in enumerate(column_peers):
        copies.append(
            pltpu.make_async_remote_copy(
                total_buf, column_buf.at[z], s2.at[k], r2.at[k],
                device_id={"seq": peer * ROW + j}, device_id_type=MESH,
            )
        )
        copies[-1].start()
    column_buf[z] = total_buf[...]
    for copy in copies:
        copy.wait()
    for head in range(2):
        state = jnp.zeros((P_SIZE, N), jnp.float32)
        for i in range(ROW - 1):
            one = decay_of(column_buf[i, head, P_SIZE:])
            after = state * one + column_buf[i, head, :P_SIZE].astype(jnp.float32)
            state = jnp.where(i < z, after, state)
        for i in range(ROW):
            back_buf[i, head] = state.astype(jnp.bfloat16)
            if i < ROW - 1:
                one = decay_of(row_buf[i, head, P_SIZE:])
                state = state * one + row_buf[i, head, :P_SIZE].astype(jnp.float32)
    copies = []
    for k, peer in enumerate(row_peers):
        copies.append(
            pltpu.make_async_remote_copy(
                back_buf.at[peer], land_buf.at[j], s3.at[k], r3.at[k],
                device_id={"seq": z * ROW + peer}, device_id_type=MESH,
            )
        )
        copies[-1].start()
    land_buf[j] = back_buf[j]
    for copy in copies:
        copy.wait()
    out_ref[...] = land_buf[...]


def chain_states(decays, states):
    high = lax.reduce_precision(decays, 8, 7)
    pair = jnp.stack([high, decays - high], axis=1)
    rows = jnp.broadcast_to(
        pair[:, :, None, None], (HG, 2, 8, N)
    ).reshape(HG, 16, N)
    mine = jnp.concatenate([states, rows], axis=1).astype(jnp.bfloat16)
    part = P_SIZE + 16
    entering = pl.pallas_call(
        states_kernel,
        out_shape=jax.ShapeDtypeStruct((ROW, 2, P_SIZE, N), jnp.bfloat16),
        in_specs=[pl.BlockSpec(memory_space=pltpu.VMEM)],
        out_specs=pl.BlockSpec(memory_space=pltpu.VMEM),
        scratch_shapes=[
            pltpu.VMEM((ROW, 2, part, N), jnp.bfloat16),
            pltpu.VMEM((2, part, N), jnp.bfloat16),
            pltpu.VMEM((ROW, 2, part, N), jnp.bfloat16),
            pltpu.VMEM((ROW, 2, P_SIZE, N), jnp.bfloat16),
            pltpu.VMEM((ROW, 2, P_SIZE, N), jnp.bfloat16),
        ]
        + [pltpu.SemaphoreType.DMA((ROW - 1,))] * 6,
        compiler_params=pltpu.CompilerParams(collective_id=0, has_side_effects=True),
        cost_estimate=pl.CostEstimate(flops=10**7, bytes_accessed=10**6, transcendentals=0),
        name="chain_states",
    )(mine.reshape(ROW, 2, part, N))
    return entering.reshape(HG, P_SIZE, N).astype(jnp.float32)


def block_local(item):
    xc, bc, cc, dtc, lc, sc = item
    cumul = jnp.cumsum(lc, axis=1)
    runs = jnp.cumsum(sc)
    tail = (
        jnp.where(
            (runs == runs[-1])[None, :], jnp.exp(jnp.minimum(cumul[:, -1:] - cumul, 0.0)), 0.0
        )
        * dtc
    )
    b_heads = jnp.repeat(bc, HG, axis=1)
    scaled = (tail[:, :, None] * jnp.swapaxes(b_heads, 0, 1).astype(jnp.float32)).astype(
        jnp.bfloat16
    )
    local = jnp.einsum("shp,hsn->hpn", xc, scaled, preferred_element_type=jnp.float32)
    total = jnp.exp(cumul[:, -1]) * (runs[-1] == 0).astype(jnp.float32)
    enter = jnp.exp(cumul) * (runs == 0).astype(jnp.float32)[None, :]
    return (local, total, enter)


def block_inner(item):
    xc, bc, cc, dtc, lc, sc = item
    length = xc.shape[0]
    cumul = jnp.cumsum(lc, axis=1)
    runs = jnp.cumsum(sc)
    lower = jnp.arange(length)[:, None] >= jnp.arange(length)[None, :]
    same = lower & (runs[:, None] == runs[None, :])
    diff = cumul[:, :, None] - cumul[:, None, :]
    wdec = jnp.where(same[None], jnp.exp(jnp.minimum(diff, 0.0)), 0.0)
    scores = jnp.einsum("tgn,sgn->gts", cc, bc, preferred_element_type=jnp.float32)
    scores_h = jnp.repeat(scores, HG, axis=0)
    weights = (scores_h * wdec * dtc[:, None, :]).astype(jnp.bfloat16)
    return jnp.einsum("hts,shp->thp", weights, xc, preferred_element_type=jnp.float32)


def body(
    xbc,
    gate_z,
    dt_raw,
    dt_bias,
    a_log,
    skip_d,
    conv_weight,
    conv_bias,
    norm_gain,
    out_weight,
    starts,
):
    tok = xbc.shape[0]
    width = conv_weight.shape[0]
    chans = xbc.shape[1]
    groups = chans // GW
    heads = dt_raw.shape[0]
    rim, rim_flags = passed_along(
        (xbc[tok - (width - 1) :], starts[tok - (width - 1) :].astype(jnp.bfloat16)), "seq", 1
    )
    flags_int = rim_flags.astype(jnp.int32)
    after_rim = jnp.sum(flags_int) - jnp.cumsum(flags_int)
    counts = jnp.cumsum(starts)
    padded = jnp.concatenate([rim, xbc], axis=0).astype(jnp.float32)
    count_ext = jnp.concatenate([-after_rim, counts])
    acc = conv_bias[None, :] + conv_weight[width - 1][None, :] * xbc.astype(jnp.float32)
    for lag in range(1, width):
        shifted = padded[width - 1 - lag : width - 1 - lag + tok]
        keep = (count_ext[width - 1 - lag : width - 1 - lag + tok] == counts).astype(jnp.float32)
        acc = acc + conv_weight[width - 1 - lag][None, :] * shifted * keep[:, None]
    unit = jax.nn.silu(acc).astype(jnp.bfloat16)
    grid = unit.reshape(tok, groups, GW)
    xs = grid[:, :, : HG * P_SIZE].reshape(tok, heads, P_SIZE)
    bmat = grid[:, :, HG * P_SIZE : HG * P_SIZE + N]
    cmat = grid[:, :, HG * P_SIZE + N :]
    steps_dt = jax.nn.softplus(dt_raw.astype(jnp.float32) + dt_bias[:, None])
    logs = -jnp.exp(a_log)[:, None] * steps_dt
    length = min(128, tok)
    nblocks = tok // length
    x_blocks = xs.reshape(nblocks, length, heads, P_SIZE)
    b_blocks = bmat.reshape(nblocks, length, groups, N)
    c_blocks = cmat.reshape(nblocks, length, groups, N)
    dt_blocks = steps_dt.reshape(heads, nblocks, length).transpose(1, 0, 2)
    log_blocks = logs.reshape(heads, nblocks, length).transpose(1, 0, 2)
    start_blocks = starts.reshape(nblocks, length)
    items = (x_blocks, b_blocks, c_blocks, dt_blocks, log_blocks, start_blocks)

    def fold(carry, item):
        local, total = item
        return ((carry[0] * total, carry[1] * total[:, None, None] + local), None)

    y_diag, (locals_all, totals, enters) = lax.map(
        lambda item: (block_inner(item), block_local(item)), items
    )
    init = (jnp.ones((heads,), jnp.float32), jnp.zeros((heads, P_SIZE, N), jnp.float32))
    result, unused = lax.scan(fold, init, (locals_all, totals))
    entering = chain_states(result[0], result[1])

    def apply(state, item):
        cc, enter, local, total = item
        c_heads = jnp.repeat(cc, HG, axis=1)
        y_off = (
            jnp.einsum(
                "thn,hpn->thp",
                c_heads,
                state.astype(jnp.bfloat16),
                preferred_element_type=jnp.float32,
            )
            * enter.T[:, :, None]
        )
        return (state * total[:, None, None] + local, y_off)

    unused_state, y_offs = lax.scan(apply, entering, (c_blocks, enters, locals_all, totals))
    y_all = (y_diag + y_offs).reshape(tok, heads, P_SIZE) + skip_d[None, :, None] * xs.astype(
        jnp.float32
    )
    gated = y_all.reshape(tok, heads * P_SIZE) * jax.nn.silu(gate_z.astype(jnp.float32))
    total_sq = lax.psum(jnp.sum(gated * gated, axis=1), "head")
    normed = (gated * lax.rsqrt(total_sq / DI + 1e-05)[:, None] * norm_gain[None, :]).astype(
        jnp.bfloat16
    )
    terms = jnp.dot(
        normed,
        lax.all_gather(out_weight, "seq", axis=1, tiled=True),
        preferred_element_type=jnp.float32,
    )
    return lax.psum_scatter(terms.astype(jnp.bfloat16), "head", scatter_dimension=1, tiled=True)


def solution(mesh):
    placed = (
        P("seq", "head"),
        P("seq", "head"),
        P("head", "seq"),
        P("head"),
        P("head"),
        P("head"),
        P(None, "head"),
        P("head"),
        P("head"),
        P("head", "seq"),
        P("seq"),
    )
    return jax.shard_map(
        body, mesh=mesh, in_specs=placed, out_specs=P("seq", "head"), check_vma=False
    )
```

```python
import jax
import jax.numpy as jnp
from jax import lax
from jax.experimental import pallas as pl
from jax.experimental.pallas import tpu as pltpu
from jax.sharding import PartitionSpec as P

P_SIZE = 64
N = 128
DI = 8192
HG = 16
GW = 1280


def passed_along(block, axis, distance):
    devices = range(lax.axis_size(axis))
    route = [(i - distance, i) for i in devices if i - distance in devices]
    return lax.ppermute(block, axis, route)


MESH = pl.DeviceIdType.MESH
ROW = 8


def decay_of(tile):
    both = tile.astype(jnp.float32)
    return both[0:1] + both[8:9]


def states_kernel(
    mine_ref, out_ref, row_buf, total_buf, column_buf, back_buf, land_buf, s1, r1, s2, r2, s3, r3
):
    place = lax.axis_index("seq")
    z = place // ROW
    j = place % ROW
    row_peers = [(j + k) % ROW for k in range(1, ROW)]
    column_peers = [(z + k) % ROW for k in range(1, ROW)]
    barrier = pltpu.get_barrier_semaphore()
    for peer in row_peers:
        pl.semaphore_signal(barrier, 1, device_id={"seq": z * ROW + peer}, device_id_type=MESH)
    for peer in column_peers:
        pl.semaphore_signal(barrier, 1, device_id={"seq": peer * ROW + j}, device_id_type=MESH)
    pl.semaphore_wait(barrier, 2 * (ROW - 1))
    copies = []
    for k, peer in enumerate(row_peers):
        copies.append(
            pltpu.make_async_remote_copy(
                mine_ref.at[peer], row_buf.at[j], s1.at[k], r1.at[k],
                device_id={"seq": z * ROW + peer}, device_id_type=MESH,
            )
        )
        copies[-1].start()
    row_buf[j] = mine_ref[j]
    for copy in copies:
        copy.wait()
    for head in range(2):
        total = row_buf[0, head, :P_SIZE].astype(jnp.float32)
        decay = decay_of(row_buf[0, head, P_SIZE:])
        for i in range(1, ROW):
            one = decay_of(row_buf[i, head, P_SIZE:])
            total = total * one + row_buf[i, head, :P_SIZE].astype(jnp.float32)
            decay = decay * one
        total_buf[head, :P_SIZE] = total.astype(jnp.bfloat16)
        high = decay.astype(jnp.bfloat16)
        low = decay - high.astype(jnp.float32)
        pair = jnp.concatenate(
            [jnp.broadcast_to(high.astype(jnp.float32), (8, N)), jnp.broadcast_to(low, (8, N))], axis=0
        )
        total_buf[head, P_SIZE:] = pair.astype(jnp.bfloat16)
    copies = []
    for k, peer in enumerate(column_peers):
        copies.append(
            pltpu.make_async_remote_copy(
                total_buf, column_buf.at[z], s2.at[k], r2.at[k],
                device_id={"seq": peer * ROW + j}, device_id_type=MESH,
            )
        )
        copies[-1].start()
    column_buf[z] = total_buf[...]
    for copy in copies:
        copy.wait()
    for head in range(2):
        state = jnp.zeros((P_SIZE, N), jnp.float32)
        for i in range(ROW - 1):
            one = decay_of(column_buf[i, head, P_SIZE:])
            after = state * one + column_buf[i, head, :P_SIZE].astype(jnp.float32)
            state = jnp.where(i < z, after, state)
        for i in range(ROW):
            back_buf[i, head] = state.astype(jnp.bfloat16)
            if i < ROW - 1:
                one = decay_of(row_buf[i, head, P_SIZE:])
                state = state * one + row_buf[i, head, :P_SIZE].astype(jnp.float32)
    copies = []
    for k, peer in enumerate(row_peers):
        copies.append(
            pltpu.make_async_remote_copy(
                back_buf.at[peer], land_buf.at[j], s3.at[k], r3.at[k],
                device_id={"seq": z * ROW + peer}, device_id_type=MESH,
            )
        )
        copies[-1].start()
    land_buf[j] = back_buf[j]
    for copy in copies:
        copy.wait()
    out_ref[...] = land_buf[...]


def chain_states(decays, states):
    high = lax.reduce_precision(decays, 8, 7)
    pair = jnp.stack([high, decays - high], axis=1)
    rows = jnp.broadcast_to(
        pair[:, :, None, None], (HG, 2, 8, N)
    ).reshape(HG, 16, N)
    mine = jnp.concatenate([states, rows], axis=1).astype(jnp.bfloat16)
    part = P_SIZE + 16
    entering = pl.pallas_call(
        states_kernel,
        out_shape=jax.ShapeDtypeStruct((ROW, 2, P_SIZE, N), jnp.bfloat16),
        in_specs=[pl.BlockSpec(memory_space=pltpu.VMEM)],
        out_specs=pl.BlockSpec(memory_space=pltpu.VMEM),
        scratch_shapes=[
            pltpu.VMEM((ROW, 2, part, N), jnp.bfloat16),
            pltpu.VMEM((2, part, N), jnp.bfloat16),
            pltpu.VMEM((ROW, 2, part, N), jnp.bfloat16),
            pltpu.VMEM((ROW, 2, P_SIZE, N), jnp.bfloat16),
            pltpu.VMEM((ROW, 2, P_SIZE, N), jnp.bfloat16),
        ]
        + [pltpu.SemaphoreType.DMA((ROW - 1,))] * 6,
        compiler_params=pltpu.CompilerParams(collective_id=0, has_side_effects=True),
        cost_estimate=pl.CostEstimate(flops=10**7, bytes_accessed=10**6, transcendentals=0),
        name="chain_states",
    )(mine.reshape(ROW, 2, part, N))
    return entering.reshape(HG, P_SIZE, N).astype(jnp.float32)


HEADS = 8
HALF = 192
COLS = 256


def project_kernel(
    mine_ref, weight_ref, square_ref, out_ref, other_buf, send_buf, recv_buf, square_buf,
    own_buf, back_buf, land_buf, a_s, a_r, send_sem, recv_sem, q_s, q_r, b_s, b_r,
):
    place = lax.axis_index("seq")
    h = lax.axis_index("head")
    core = place % 2
    partner = place + 1 - 2 * core
    ways = ((h + 1) % HEADS, (h + HEADS - 1) % HEADS)
    peers = [(h + k) % HEADS for k in range(1, HEADS)]
    barrier = pltpu.get_barrier_semaphore()
    pl.semaphore_signal(barrier, 1, device_id={"seq": partner}, device_id_type=MESH)
    for peer in peers:
        pl.semaphore_signal(barrier, 1, device_id={"head": peer}, device_id_type=MESH)
    pl.semaphore_wait(barrier, HEADS)
    swap = pltpu.make_async_remote_copy(
        mine_ref, other_buf, a_s, a_r, device_id={"seq": partner}, device_id_type=MESH
    )
    swap.start()
    tokens = (mine_ref, other_buf)

    def partial(step, way, side):
        chunk = (h + 2 * HEADS - 1 - step) % HEADS if way == 0 else (h + 1 + step) % HEADS
        start = pl.multiple_of(chunk * COLS, COLS)
        return lax.dot_general(
            tokens[side][way * HALF : (way + 1) * HALF, :],
            weight_ref[pl.ds(start, COLS), :],
            (((1,), (1,)), ((), ())),
            preferred_element_type=jnp.float32,
        )

    def hop(step, way, side):
        return pltpu.make_async_remote_copy(
            send_buf.at[step, way, side], recv_buf.at[step, way, side],
            send_sem.at[step, way, side], recv_sem.at[step, way, side],
            device_id={"head": ways[way]}, device_id_type=MESH,
        )

    def summed(step, way, side):
        term = partial(step, way, side)
        hop(step - 1, way, side).wait_recv()
        return term + recv_buf[step - 1, way, side].astype(jnp.float32)

    for way in range(2):
        send_buf[0, way, 0] = partial(0, way, 0).astype(jnp.bfloat16)
        hop(0, way, 0).start()
    squares = []
    for k, peer in enumerate(peers):
        squares.append(
            pltpu.make_async_remote_copy(
                square_ref, square_buf.at[h], q_s.at[k], q_r.at[k],
                device_id={"head": peer}, device_id_type=MESH,
            )
        )
        squares[-1].start()
    square_buf[h] = square_ref[...]
    swap.wait()
    for way in range(2):
        send_buf[0, way, 1] = partial(0, way, 1).astype(jnp.bfloat16)
        hop(0, way, 1).start()

    def one(step, carry):
        for side in range(2):
            for way in range(2):
                send_buf[step, way, side] = summed(step, way, side).astype(jnp.bfloat16)
                hop(step, way, side).start()
        return carry

    lax.fori_loop(1, HEADS - 1, one, 0)
    last = HEADS - 1
    for way in range(2):
        own_buf[way * HALF : (way + 1) * HALF, :] = summed(last, way, 0)
    backs = []
    for way in range(2):
        rows = pl.ds(way * HALF, HALF)
        back_buf[way * HALF : (way + 1) * HALF, :] = summed(last, way, 1).astype(jnp.bfloat16)
        backs.append(
            pltpu.make_async_remote_copy(
                back_buf.at[rows], land_buf.at[rows], b_s.at[way], b_r.at[way],
                device_id={"seq": partner}, device_id_type=MESH,
            )
        )
        backs[-1].start()
    for copy in squares:
        copy.wait()
    total = square_buf[0]
    for k in range(1, HEADS):
        total = total + square_buf[k]
    scale = lax.rsqrt(total / DI + 1e-05)
    scale = jnp.concatenate([scale] * 16, axis=0).T
    for copy in backs:
        copy.wait()
    for part in range(3):
        rows = slice(part * 128, (part + 1) * 128)
        factor = jnp.broadcast_to(scale[:, part : part + 1], (128, 128))
        own = own_buf[rows, :]
        other = land_buf[rows, :].astype(jnp.float32)
        for x in range(4):
            mine = own[:, x * 64 : (x + 1) * 64]
            theirs = other[:, x * 64 : (x + 1) * 64]
            block = jnp.where(
                core == 0,
                jnp.concatenate([mine, theirs], axis=1),
                jnp.concatenate([theirs, mine], axis=1),
            )
            out_ref[rows, x * 128 : (x + 1) * 128] = (block * factor).astype(jnp.bfloat16)

    def drain(step, carry):
        for side in range(2):
            for way in range(2):
                hop(step, way, side).wait_send()
        return carry

    lax.fori_loop(0, HEADS - 1, drain, 0)


def project(gained, weight, squares):
    steps = HEADS - 1
    return pl.pallas_call(
        project_kernel,
        out_shape=jax.ShapeDtypeStruct((2 * HALF, 2 * COLS), jnp.bfloat16),
        in_specs=[pl.BlockSpec(memory_space=pltpu.VMEM)] * 3,
        out_specs=pl.BlockSpec(memory_space=pltpu.VMEM),
        scratch_shapes=[
            pltpu.VMEM((2 * HALF, 1024), jnp.bfloat16),
            pltpu.VMEM((steps, 2, 2, HALF, COLS), jnp.bfloat16),
            pltpu.VMEM((steps, 2, 2, HALF, COLS), jnp.bfloat16),
            pltpu.VMEM((HEADS, 8, 128), jnp.float32),
            pltpu.VMEM((2 * HALF, COLS), jnp.float32),
            pltpu.VMEM((2 * HALF, COLS), jnp.bfloat16),
            pltpu.VMEM((2 * HALF, COLS), jnp.bfloat16),
            pltpu.SemaphoreType.DMA,
            pltpu.SemaphoreType.DMA,
            pltpu.SemaphoreType.DMA((steps, 2, 2)),
            pltpu.SemaphoreType.DMA((steps, 2, 2)),
            pltpu.SemaphoreType.DMA((steps,)),
            pltpu.SemaphoreType.DMA((steps,)),
            pltpu.SemaphoreType.DMA((2,)),
            pltpu.SemaphoreType.DMA((2,)),
        ],
        compiler_params=pltpu.CompilerParams(collective_id=1, has_side_effects=True),
        cost_estimate=pl.CostEstimate(flops=4 * 10**9, bytes_accessed=10**7, transcendentals=0),
        name="project",
    )(gained, weight, squares)


def block_local(item):
    xc, bc, cc, dtc, lc, sc = item
    cumul = jnp.cumsum(lc, axis=1)
    runs = jnp.cumsum(sc)
    tail = (
        jnp.where(
            (runs == runs[-1])[None, :], jnp.exp(jnp.minimum(cumul[:, -1:] - cumul, 0.0)), 0.0
        )
        * dtc
    )
    b_heads = jnp.repeat(bc, HG, axis=1)
    scaled = (tail[:, :, None] * jnp.swapaxes(b_heads, 0, 1).astype(jnp.float32)).astype(
        jnp.bfloat16
    )
    local = jnp.einsum("shp,hsn->hpn", xc, scaled, preferred_element_type=jnp.float32)
    total = jnp.exp(cumul[:, -1]) * (runs[-1] == 0).astype(jnp.float32)
    enter = jnp.exp(cumul) * (runs == 0).astype(jnp.float32)[None, :]
    return (local, total, enter)


def block_inner(item):
    xc, bc, cc, dtc, lc, sc = item
    length = xc.shape[0]
    cumul = jnp.cumsum(lc, axis=1)
    runs = jnp.cumsum(sc)
    lower = jnp.arange(length)[:, None] >= jnp.arange(length)[None, :]
    same = lower & (runs[:, None] == runs[None, :])
    diff = cumul[:, :, None] - cumul[:, None, :]
    wdec = jnp.where(same[None], jnp.exp(jnp.minimum(diff, 0.0)), 0.0)
    scores = jnp.einsum("tgn,sgn->gts", cc, bc, preferred_element_type=jnp.float32)
    scores_h = jnp.repeat(scores, HG, axis=0)
    weights = (scores_h * wdec * dtc[:, None, :]).astype(jnp.bfloat16)
    return jnp.einsum("hts,shp->thp", weights, xc, preferred_element_type=jnp.float32)


def body(
    xbc,
    gate_z,
    dt_raw,
    dt_bias,
    a_log,
    skip_d,
    conv_weight,
    conv_bias,
    norm_gain,
    out_weight,
    starts,
):
    tok = xbc.shape[0]
    cores = [[2 * i + c for i in range(lax.axis_size("seq") // 2)] for c in range(2)]
    weight = lax.all_gather(out_weight.T, "seq", axis_index_groups=cores, axis=0, tiled=True)
    width = conv_weight.shape[0]
    chans = xbc.shape[1]
    groups = chans // GW
    heads = dt_raw.shape[0]
    rim, rim_flags = passed_along(
        (xbc[tok - (width - 1) :], starts[tok - (width - 1) :].astype(jnp.bfloat16)), "seq", 1
    )
    flags_int = rim_flags.astype(jnp.int32)
    after_rim = jnp.sum(flags_int) - jnp.cumsum(flags_int)
    counts = jnp.cumsum(starts)
    padded = jnp.concatenate([rim, xbc], axis=0).astype(jnp.float32)
    count_ext = jnp.concatenate([-after_rim, counts])
    acc = conv_bias[None, :] + conv_weight[width - 1][None, :] * xbc.astype(jnp.float32)
    for lag in range(1, width):
        shifted = padded[width - 1 - lag : width - 1 - lag + tok]
        keep = (count_ext[width - 1 - lag : width - 1 - lag + tok] == counts).astype(jnp.float32)
        acc = acc + conv_weight[width - 1 - lag][None, :] * shifted * keep[:, None]
    unit = jax.nn.silu(acc).astype(jnp.bfloat16)
    grid = unit.reshape(tok, groups, GW)
    xs = grid[:, :, : HG * P_SIZE].reshape(tok, heads, P_SIZE)
    bmat = grid[:, :, HG * P_SIZE : HG * P_SIZE + N]
    cmat = grid[:, :, HG * P_SIZE + N :]
    steps_dt = jax.nn.softplus(dt_raw.astype(jnp.float32) + dt_bias[:, None])
    logs = -jnp.exp(a_log)[:, None] * steps_dt
    length = min(128, tok)
    nblocks = tok // length
    x_blocks = xs.reshape(nblocks, length, heads, P_SIZE)
    b_blocks = bmat.reshape(nblocks, length, groups, N)
    c_blocks = cmat.reshape(nblocks, length, groups, N)
    dt_blocks = steps_dt.reshape(heads, nblocks, length).transpose(1, 0, 2)
    log_blocks = logs.reshape(heads, nblocks, length).transpose(1, 0, 2)
    start_blocks = starts.reshape(nblocks, length)
    items = (x_blocks, b_blocks, c_blocks, dt_blocks, log_blocks, start_blocks)

    def fold(carry, item):
        local, total = item
        return ((carry[0] * total, carry[1] * total[:, None, None] + local), None)

    y_diag, (locals_all, totals, enters) = lax.map(
        lambda item: (block_inner(item), block_local(item)), items
    )
    init = (jnp.ones((heads,), jnp.float32), jnp.zeros((heads, P_SIZE, N), jnp.float32))
    result, unused = lax.scan(fold, init, (locals_all, totals))
    entering = chain_states(result[0], result[1])

    def apply(state, item):
        cc, enter, local, total = item
        c_heads = jnp.repeat(cc, HG, axis=1)
        y_off = (
            jnp.einsum(
                "thn,hpn->thp",
                c_heads,
                state.astype(jnp.bfloat16),
                preferred_element_type=jnp.float32,
            )
            * enter.T[:, :, None]
        )
        return (state * total[:, None, None] + local, y_off)

    unused_state, y_offs = lax.scan(apply, entering, (c_blocks, enters, locals_all, totals))
    y_all = (y_diag + y_offs).reshape(tok, heads, P_SIZE) + skip_d[None, :, None] * xs.astype(
        jnp.float32
    )
    gated = y_all.reshape(tok, heads * P_SIZE) * jax.nn.silu(gate_z.astype(jnp.float32))
    squares = jnp.sum(gated * gated, axis=1).reshape(tok // 128, 128)
    squares = jnp.pad(squares, ((0, 8 - tok // 128), (0, 0)))
    gained = (gated * norm_gain[None, :]).astype(jnp.bfloat16)
    return project(gained, weight, squares)


def solution(mesh):
    placed = (
        P("seq", "head"),
        P("seq", "head"),
        P("head", "seq"),
        P("head"),
        P("head"),
        P("head"),
        P(None, "head"),
        P("head"),
        P("head"),
        P("head", "seq"),
        P("seq"),
    )
    return jax.shard_map(
        body, mesh=mesh, in_specs=placed, out_specs=P("seq", "head"), check_vma=False
    )
```

```python
import jax
import jax.numpy as jnp
from jax import lax
from jax.experimental import pallas as pl
from jax.experimental.pallas import tpu as pltpu
from jax.sharding import PartitionSpec as P

MESH = pl.DeviceIdType.MESH
P_SIZE = 64
N = 128
DI = 8192
HG = 16
GW = 1280
TOK = 384
RIM = 16
WIDTH = HG * P_SIZE
PART = P_SIZE + 16
ROW = 8
HEADS = 8
HALF = 192
COLS = 256
BF = jnp.bfloat16
F32 = jnp.float32
SHAPES = dict(
    halo=((RIM, GW), BF),
    halo_starts=((8, N), F32),
    ext=((RIM + TOK, GW), F32),
    flags=((RIM + TOK, N), F32),
    keep=((3, TOK, N), F32),
    unit=((TOK, GW), BF),
    spread=((N, WIDTH), BF),
    scaled=((TOK, WIDTH), BF),
    linear=((TOK, WIDTH), F32),
    enter=((TOK, N), BF),
    masked_c=((TOK, N), BF),
    mine=((ROW, 2, PART, N), BF),
    row=((ROW, 2, PART, N), BF),
    total=((2, PART, N), BF),
    column=((ROW, 2, PART, N), BF),
    back=((ROW, 2, P_SIZE, N), BF),
    land=((ROW, 2, P_SIZE, N), BF),
    weight=((HEADS, COLS, WIDTH), BF),
    gained=((TOK, WIDTH), BF),
    other=((TOK, WIDTH), BF),
    send=((HEADS - 1, 2, 2, HALF, COLS), BF),
    recv=((HEADS - 1, 2, 2, HALF, COLS), BF),
    square=((8, N), F32),
    squares=((HEADS, 8, N), F32),
    own=((TOK, COLS), F32),
    home=((TOK, COLS), BF),
    home_land=((TOK, COLS), BF),
)
SEMS = dict(
    halo=(2,), wx=(3,), wz=(4, 2), rows=(7,), columns=(7,), backs=(7,),
    swap=(1,), ring=(HEADS - 1, 2, 2), square=(7,), home=(2,),
)


def dot(a, b, ca=1, cb=0):
    return lax.dot_general(a, b, (((ca,), (cb,)), ((), ())), preferred_element_type=F32)


def iota(shape, axis):
    return lax.broadcasted_iota(jnp.int32, shape, axis)


def split_lanes(value, axis):
    high = value.astype(BF).astype(F32)
    index = iota(value.shape, axis)
    pair = jnp.where(index < HG, high, jnp.where(index < 2 * HG, value - high, 0.0))
    return pair.astype(BF)


def decay_of(tile):
    both = tile.astype(F32)
    return both[0:1] + both[8:9]


def decay_rows(decay):
    high = decay.astype(BF).astype(F32)
    return jnp.concatenate([high, decay - high], axis=0).astype(BF)


def columns_of(rows):
    return jnp.concatenate([rows] * (N // rows.shape[0]), axis=0).T


def layer_kernel(
    xbc_ref, gate_ref, dt_ref, bias_ref, log_ref, skip_ref, taps_ref, shift_ref, gain_ref,
    weight_ref, starts_ref, out_ref, *scratch,
):
    names = list(SHAPES)
    b = dict(zip(names, scratch[: len(names)]))
    sems = scratch[len(names) :]
    ss = dict(zip(SEMS, sems[: len(SEMS)]))
    rs = dict(zip(SEMS, sems[len(SEMS) :]))
    place = lax.axis_index("seq")
    h = lax.axis_index("head")
    z = place // ROW
    j = place % ROW
    x = j // 2
    core = j % 2
    partner = place + 1 - 2 * core
    after = (place + 1) % 64
    before = (place + 63) % 64
    row_peers = [z * ROW + (j + k) % ROW for k in range(1, ROW)]
    column_peers = [((z + k) % ROW) * ROW + j for k in range(1, ROW)]
    head_peers = [(h + k) % HEADS for k in range(1, HEADS)]
    ways = (head_peers[0], head_peers[-1])

    barrier = pltpu.get_barrier_semaphore()
    for peer in row_peers + column_peers + [after, before]:
        pl.semaphore_signal(barrier, 1, device_id={"seq": peer}, device_id_type=MESH)
    for peer in head_peers:
        pl.semaphore_signal(barrier, 1, device_id={"head": peer}, device_id_type=MESH)
    pl.semaphore_wait(barrier, 23)

    def copy(src, dst, name, at, axis, peer):
        return pltpu.make_async_remote_copy(
            src, dst, ss[name].at[at], rs[name].at[at],
            device_id={axis: peer}, device_id_type=MESH,
        )

    halo = [
        copy(xbc_ref.at[pl.ds(TOK - RIM, RIM)], b["halo"], "halo", 0, "seq", after),
        copy(starts_ref.at[:, pl.ds(TOK - N, N)], b["halo_starts"], "halo", 1, "seq", after),
    ]
    for one in halo:
        one.start()
    block = pl.ds(pl.multiple_of(x * 64, 64), 64)
    around = []
    for k in range(1, 4):
        peer = z * ROW + ((x + k) % 4) * 2 + core
        around.append(copy(weight_ref, b["weight"].at[z, block], "wx", k - 1, "seq", peer))
        around[-1].start()
    b["weight"][z, block] = weight_ref[...]

    def pass_on(step):
        up = (z + 9 - step) % ROW
        down = (z + step - 1) % ROW
        rows = (pl.ds(0, COLS), pl.ds(0, COLS))
        if step == 4:
            rows = (pl.ds(0, COLS // 2), pl.ds(COLS // 2, COLS // 2))
        pair = []
        for way, (chunk, peer) in enumerate(((up, column_peers[0]), (down, column_peers[-1]))):
            part = b["weight"].at[chunk, rows[way]]
            pair.append(copy(part, part, "wz", (step - 1, way), "seq", peer))
            pair[-1].start()
        return pair

    starts = starts_ref[...]
    lower = iota((TOK, TOK), 0) >= iota((TOK, TOK), 1)
    tri = jnp.where(lower, 1.0, 0.0).astype(BF)
    flag_col = columns_of(starts)
    dt_row = dt_ref[...].astype(F32) + jnp.concatenate([bias_ref[...]] * 3, axis=1)
    dt_row = jnp.maximum(dt_row, 0.0) + jnp.log1p(jnp.exp(-jnp.abs(dt_row)))
    dt_col = columns_of(dt_row)
    log_col = columns_of(-jnp.exp(jnp.concatenate([log_ref[...]] * 3, axis=1)) * dt_row)
    log_high = log_col.astype(BF)
    log_low = (log_col - log_high.astype(F32)).astype(BF)
    cumul = dot(tri, log_high) + dot(tri, log_low)
    runs = dot(tri, flag_col.astype(BF))
    runs_row = dot(starts.astype(BF), tri, 1, 1)
    growth = jnp.exp(cumul)
    b["enter"][...] = split_lanes(growth, 1)
    inverse = split_lanes(jnp.exp(-cumul) * dt_col, 1)
    low_index = iota((N, WIDTH), 0)
    spread = (low_index < 2 * HG) & ((low_index & (HG - 1)) == (iota((N, WIDTH), 1) >> 6))
    b["spread"][...] = jnp.where(spread, 1.0, 0.0).astype(BF)

    for one in halo:
        one.wait()
    real = jnp.where(place > 0, 1.0, 0.0)
    b["ext"][:RIM] = b["halo"][...].astype(F32) * real
    b["ext"][RIM:] = xbc_ref[...].astype(F32)
    b["flags"][:RIM] = columns_of(b["halo_starts"][...])[N - RIM :] * real
    b["flags"][RIM:] = flag_col
    crossed = b["flags"][RIM:]
    for lag in range(1, 4):
        b["keep"][lag - 1] = jnp.where(crossed == 0.0, 1.0, 0.0)
        crossed = crossed + b["flags"][RIM - lag : RIM - lag + TOK]

    def conv(c, carry):
        lanes = pl.ds(pl.multiple_of(c * N, N), N)
        acc = shift_ref[:, lanes] + taps_ref[3:4, lanes] * b["ext"][RIM:, lanes]
        for lag in range(1, 4):
            early = b["ext"][pl.ds(RIM - lag, TOK), lanes]
            acc = acc + taps_ref[3 - lag : 4 - lag, lanes] * early * b["keep"][lag - 1]
        b["unit"][:, lanes] = (acc / (1.0 + jnp.exp(-acc))).astype(BF)
        return carry

    lax.fori_loop(0, GW // N, conv, 0)
    for one in around:
        one.wait()
    moved = [pass_on(1)]

    for c in range(WIDTH // N):
        lanes = slice(c * N, (c + 1) * N)
        factor = dot(inverse, b["spread"][:, lanes])
        b["scaled"][:, lanes] = (b["unit"][:, lanes].astype(F32) * factor).astype(BF)
    bmat = b["unit"][:, WIDTH : WIDTH + N]
    cmat = b["unit"][:, WIDTH + N :]
    last = runs[TOK - 1 : TOK, :]
    tail_b = jnp.where(runs == last, bmat.astype(F32), 0.0).astype(BF)
    state = dot(b["scaled"][...], tail_b, 0, 0)
    ends = jnp.broadcast_to(growth[TOK - 1 : TOK, :], (N, N)).T
    ends = dot(b["spread"][...], split_lanes(ends, 0), 0, 0)
    state = state * ends
    unbroken = jnp.where(last == 0.0, 1.0, 0.0)
    for head in range(HG):
        at = head * P_SIZE
        b["mine"][head // 2, head % 2, :P_SIZE] = state[at : at + P_SIZE].astype(BF)
        b["mine"][head // 2, head % 2, P_SIZE:] = decay_rows(ends[at : at + 8] * unbroken)
    copies = []
    for k in range(1, ROW):
        to = (j + k) % ROW
        copies.append(copy(b["mine"].at[to], b["row"].at[j], "rows", k - 1, "seq", row_peers[k - 1]))
        copies[-1].start()
    b["row"][j] = b["mine"][j]
    scores = dot(cmat, bmat, 1, 1)
    same = lower & (jnp.concatenate([runs] * 3, axis=1) == runs_row[0:1])
    scores = jnp.where(same, scores, 0.0).astype(BF)
    b["masked_c"][...] = jnp.where(runs == 0.0, cmat.astype(F32), 0.0).astype(BF)
    for c in range(4):
        lanes = slice(c * COLS, (c + 1) * COLS)
        b["linear"][:, lanes] = dot(scores, b["scaled"][:, lanes])
    for one in copies:
        one.wait()

    for head in range(2):
        total = b["row"][0, head, :P_SIZE].astype(F32)
        decay = decay_of(b["row"][0, head, P_SIZE:])
        for i in range(1, ROW):
            one = decay_of(b["row"][i, head, P_SIZE:])
            total = total * one + b["row"][i, head, :P_SIZE].astype(F32)
            decay = decay * one
        b["total"][head, :P_SIZE] = total.astype(BF)
        b["total"][head, P_SIZE:] = decay_rows(jnp.broadcast_to(decay, (8, N)))
    copies = []
    for k, peer in enumerate(column_peers):
        copies.append(copy(b["total"], b["column"].at[z], "columns", k, "seq", peer))
        copies[-1].start()
    b["column"][z] = b["total"][...]
    for step in (2,):
        for one in moved[-1]:
            one.wait_recv()
        moved.append(pass_on(step))
    for one in copies:
        one.wait()
    for head in range(2):
        state = jnp.zeros((P_SIZE, N), F32)
        for i in range(ROW - 1):
            one = decay_of(b["column"][i, head, P_SIZE:])
            later = state * one + b["column"][i, head, :P_SIZE].astype(F32)
            state = jnp.where(i < z, later, state)
        for i in range(ROW):
            b["back"][i, head] = state.astype(BF)
            if i < ROW - 1:
                one = decay_of(b["row"][i, head, P_SIZE:])
                state = state * one + b["row"][i, head, :P_SIZE].astype(F32)
    copies = []
    for k in range(1, ROW):
        to = (j + k) % ROW
        copies.append(copy(b["back"].at[to], b["land"].at[j], "backs", k - 1, "seq", row_peers[k - 1]))
        copies[-1].start()
    b["land"][j] = b["back"][j]
    for one in moved[-1]:
        one.wait_recv()
    moved.append(pass_on(3))
    for one in copies:
        one.wait()

    square = jnp.zeros((TOK, N), F32)
    for c in range(WIDTH // N):
        lanes = slice(c * N, (c + 1) * N)
        state = b["land"][c].reshape(N, N)
        y = b["linear"][:, lanes] + dot(b["masked_c"][...], state, 1, 1)
        y = y * dot(b["enter"][...], b["spread"][:, lanes])
        y = y + skip_ref[:, lanes] * b["unit"][:, lanes].astype(F32)
        gate = gate_ref[:, lanes].astype(F32)
        gated = y * (gate / (1.0 + jnp.exp(-gate)))
        square = square + gated * gated
        b["gained"][:, lanes] = (gated * gain_ref[:, lanes]).astype(BF)
    square = jnp.sum(square.T, axis=0, keepdims=True)
    b["square"][...] = jnp.concatenate(
        [square[:, i * N : (i + 1) * N] for i in range(3)] + [jnp.zeros((5, N), F32)], axis=0
    )

    swap = copy(b["gained"], b["other"], "swap", 0, "seq", partner)
    swap.start()
    for one in moved[-1]:
        one.wait_recv()
    moved.append(pass_on(4))
    squares = []
    for k, peer in enumerate(head_peers):
        squares.append(copy(b["square"], b["squares"].at[h], "square", k, "head", peer))
        squares[-1].start()
    b["squares"][h] = b["square"][...]
    for one in moved[-1]:
        one.wait_recv()
    tokens = (b["gained"], b["other"])

    def partial(step, way, side):
        chunk = (h + 2 * HEADS - 1 - step) % HEADS if way == 0 else (h + 1 + step) % HEADS
        return dot(tokens[side][way * HALF : (way + 1) * HALF, :], b["weight"][chunk], 1, 1)

    def hop(step, way, side):
        at = (step, way, side)
        return copy(b["send"].at[at], b["recv"].at[at], "ring", at, "head", ways[way])

    def summed(step, way, side):
        term = partial(step, way, side)
        hop(step - 1, way, side).wait_recv()
        return term + b["recv"][step - 1, way, side].astype(F32)

    for side in range(2):
        if side == 1:
            swap.wait()
        for way in range(2):
            b["send"][0, way, side] = partial(0, way, side).astype(BF)
            hop(0, way, side).start()

    def one_step(step, carry):
        for side in range(2):
            for way in range(2):
                b["send"][step, way, side] = summed(step, way, side).astype(BF)
                hop(step, way, side).start()
        return carry

    lax.fori_loop(1, HEADS - 1, one_step, 0)
    final = HEADS - 1
    for way in range(2):
        b["own"][way * HALF : (way + 1) * HALF, :] = summed(final, way, 0)
    homes = []
    for way in range(2):
        rows = pl.ds(way * HALF, HALF)
        b["home"][way * HALF : (way + 1) * HALF, :] = summed(final, way, 1).astype(BF)
        homes.append(
            copy(b["home"].at[rows], b["home_land"].at[rows], "home", way, "seq", partner)
        )
        homes[-1].start()
    for one in squares:
        one.wait()
    total = b["squares"][0]
    for k in range(1, HEADS):
        total = total + b["squares"][k]
    scale = columns_of(lax.rsqrt(total / DI + 1e-05))
    for one in homes:
        one.wait()
    for part in range(3):
        rows = slice(part * N, (part + 1) * N)
        factor = jnp.broadcast_to(scale[:, part : part + 1], (N, N))
        own = b["own"][rows, :]
        other = b["home_land"][rows, :].astype(F32)
        for i in range(4):
            mine = own[:, i * 64 : (i + 1) * 64]
            theirs = other[:, i * 64 : (i + 1) * 64]
            block = jnp.where(
                core == 0,
                jnp.concatenate([mine, theirs], axis=1),
                jnp.concatenate([theirs, mine], axis=1),
            )
            out_ref[rows, i * N : (i + 1) * N] = (block * factor).astype(BF)

    def drain(step, carry):
        for side in range(2):
            for way in range(2):
                hop(step, way, side).wait_send()
        return carry

    lax.fori_loop(0, HEADS - 1, drain, 0)
    for pair in moved:
        for one in pair:
            one.wait_send()


def body(
    xbc,
    gate_z,
    dt_raw,
    dt_bias,
    a_log,
    skip_d,
    conv_weight,
    conv_bias,
    norm_gain,
    out_weight,
    starts,
):
    flags = jnp.broadcast_to(starts.astype(F32)[None, :], (8, TOK))
    bias = jnp.broadcast_to(dt_bias[:, None], (HG, N))
    logs = jnp.broadcast_to(a_log[:, None], (HG, N))
    skip = jnp.broadcast_to(skip_d[:, None], (HG, P_SIZE)).reshape(1, WIDTH)
    sems = [pltpu.SemaphoreType.DMA(shape) for shape in SEMS.values()]
    return pl.pallas_call(
        layer_kernel,
        out_shape=jax.ShapeDtypeStruct((TOK, 2 * COLS), BF),
        in_specs=[pl.BlockSpec(memory_space=pltpu.VMEM)] * 11,
        out_specs=pl.BlockSpec(memory_space=pltpu.VMEM),
        scratch_shapes=[pltpu.VMEM(*spec) for spec in SHAPES.values()] + sems + sems,
        compiler_params=pltpu.CompilerParams(collective_id=0, has_side_effects=True),
        name="layer",
    )(
        xbc, gate_z, dt_raw, bias, logs, skip, conv_weight, conv_bias[None, :],
        norm_gain[None, :], out_weight.T, flags,
    )


def solution(mesh):
    placed = (
        P("seq", "head"),
        P("seq", "head"),
        P("head", "seq"),
        P("head"),
        P("head"),
        P("head"),
        P(None, "head"),
        P("head"),
        P("head"),
        P("head", "seq"),
        P("seq"),
    )
    return jax.shard_map(
        body, mesh=mesh, in_specs=placed, out_specs=P("seq", "head"), check_vma=False
    )
```

```python
import jax
import jax.numpy as jnp
from jax import lax
from jax.experimental import pallas as pl
from jax.experimental.pallas import tpu as pltpu
from jax.sharding import PartitionSpec as P

MESH = pl.DeviceIdType.MESH
P_SIZE = 64
N = 128
DI = 8192
HG = 16
GW = 1280
TOK = 384
RIM = 16
WIDTH = HG * P_SIZE
PART = P_SIZE + 16
ROW = 8
HEADS = 8
HALF = 192
PIECE = 96
COLS = 256
BF = jnp.bfloat16
F32 = jnp.float32
SHAPES = dict(
    halo=((RIM, GW), BF),
    halo_starts=((8, N), F32),
    starts=((8, TOK), F32),
    skip=((8, WIDTH), F32),
    ext=((RIM + TOK, GW), F32),
    flags=((RIM + TOK, N), F32),
    keep=((3, TOK, N), F32),
    unit=((TOK, GW), BF),
    spread=((N, WIDTH), BF),
    scaled=((TOK, WIDTH), BF),
    linear=((TOK, WIDTH), F32),
    enter=((TOK, N), BF),
    masked_c=((TOK, N), BF),
    mine=((ROW, 2, PART, N), BF),
    row=((ROW, 2, PART, N), BF),
    total=((2, PART, N), BF),
    column=((ROW, 2, PART, N), BF),
    back=((ROW, 2, P_SIZE, N), BF),
    land=((ROW, 2, P_SIZE, N), BF),
    weight_a=((HEADS, COLS, WIDTH // 2), BF),
    weight_b=((HEADS, COLS, WIDTH // 2), BF),
    gained=((TOK, WIDTH), BF),
    other=((TOK, WIDTH), BF),
    send=((HEADS - 1, 2, 2, 2, PIECE, COLS), BF),
    recv=((HEADS - 1, 2, 2, 2, PIECE, COLS), BF),
    terms=((2, 2, HALF, COLS), F32),
    square=((8, N), F32),
    squares=((HEADS, 8, N), F32),
    own=((TOK, COLS), F32),
    home=((TOK, COLS), BF),
    home_land=((TOK, COLS), BF),
)
SEMS = dict(
    halo=(2,), ax=(3,), az=(4, 2), bz=(4, 2), bx=(ROW, 3), rows=(7,), columns=(7,), backs=(7,),
    swap=(1,), ring=(HEADS - 1, 2, 2, 2), square=(7,), home=(4,),
)


def dot(a, b, ca=1, cb=0):
    return lax.dot_general(a, b, (((ca,), (cb,)), ((), ())), preferred_element_type=F32)


def iota(shape, axis):
    return lax.broadcasted_iota(jnp.int32, shape, axis)


def split_lanes(value, axis):
    high = value.astype(BF).astype(F32)
    index = iota(value.shape, axis)
    pair = jnp.where(index < HG, high, jnp.where(index < 2 * HG, value - high, 0.0))
    return pair.astype(BF)


def decay_of(tile):
    both = tile.astype(F32)
    return both[0:1] + both[8:9]


def decay_rows(decay):
    high = decay.astype(BF).astype(F32)
    return jnp.concatenate([high, decay - high], axis=0).astype(BF)


def two_terms(value):
    high = value.astype(BF).astype(F32)
    return high + (value - high).astype(BF).astype(F32)


def across(ref):
    return jnp.concatenate([ref[...]] * (N // HG), axis=1)


def columns_of(rows):
    return jnp.concatenate([rows] * (N // rows.shape[0]), axis=0).T


def layer_kernel(
    xbc_ref, gate_ref, dt_ref, bias_ref, log_ref, skip_ref, taps_ref, shift_ref, gain_ref,
    weight_ref, starts_ref, out_ref, *scratch,
):
    names = list(SHAPES)
    b = dict(zip(names, scratch[: len(names)]))
    sems = scratch[len(names) :]
    ss = dict(zip(SEMS, sems[: len(SEMS)]))
    rs = dict(zip(SEMS, sems[len(SEMS) :]))
    place = lax.axis_index("seq")
    h = lax.axis_index("head")
    z = place // ROW
    j = place % ROW
    x = j // 2
    core = j % 2
    partner = place + 1 - 2 * core
    after = (place + 1) % 64
    before = (place + 63) % 64
    row_peers = [z * ROW + (j + k) % ROW for k in range(1, ROW)]
    column_peers = [((z + k) % ROW) * ROW + j for k in range(1, ROW)]
    head_peers = [(h + k) % HEADS for k in range(1, HEADS)]
    ways = (head_peers[0], head_peers[-1])

    barrier = pltpu.get_barrier_semaphore()
    for peer in row_peers + column_peers + [after, before]:
        pl.semaphore_signal(barrier, 1, device_id={"seq": peer}, device_id_type=MESH)
    for peer in head_peers:
        pl.semaphore_signal(barrier, 1, device_id={"head": peer}, device_id_type=MESH)

    def copy(src, dst, name, at, axis, peer):
        return pltpu.make_async_remote_copy(
            src, dst, ss[name].at[at], rs[name].at[at],
            device_id={axis: peer}, device_id_type=MESH,
        )

    block = pl.ds(pl.multiple_of(x * 64, 64), 64)
    halves = (pl.ds(0, WIDTH // 2), pl.ds(WIDTH // 2, WIDTH // 2))
    side_peers = [z * ROW + ((x + k) % 4) * 2 + core for k in range(1, 4)]
    sideways = []

    def fan(turn):
        chunk = (z + turn) % ROW
        part = b["weight_b"].at[chunk, block]
        source = weight_ref.at[:, halves[1]] if turn == 0 else part
        for k, peer in enumerate(side_peers):
            sideways.append(copy(source, part, "bx", (turn, k), "seq", peer))
            sideways[-1].start()

    def pass_on(name, step):
        pair = []
        for way, peer in enumerate((column_peers[0], column_peers[-1])):
            chunk = (z + 9 - step) % ROW if way == 0 else (z + step - 1) % ROW
            first, count = (0, COLS) if name == "az" else (x * 64, 64)
            if step == 4:
                count = count // 2
                first = first + way * count
            rows = pl.ds(pl.multiple_of(first, count), count)
            part = b["weight_a" if name == "az" else "weight_b"].at[chunk, rows]
            source = part
            if name == "bz" and step == 1:
                source = weight_ref.at[:, halves[1]]
            pair.append(copy(source, part, name, (step - 1, way), "seq", peer))
            pair[-1].start()
        return pair

    def arrived(pair):
        for one in pair:
            one.wait_recv()

    starts = jnp.broadcast_to(starts_ref[...].astype(F32)[None, :], (8, TOK))
    b["starts"][...] = starts
    lower = iota((TOK, TOK), 0) >= iota((TOK, TOK), 1)
    tri = jnp.where(lower, 1.0, 0.0).astype(BF)
    flag_col = columns_of(starts)
    pl.semaphore_wait(barrier, 23)
    halo = [
        copy(xbc_ref.at[pl.ds(TOK - RIM, RIM)], b["halo"], "halo", 0, "seq", after),
        copy(
            b["starts"].at[:, pl.ds(TOK - N, N)], b["halo_starts"], "halo", 1, "seq", after
        ),
    ]
    for one in halo:
        one.start()
    around = []
    for k, peer in enumerate(side_peers):
        part = b["weight_a"].at[z, block]
        around.append(copy(weight_ref.at[:, halves[0]], part, "ax", k, "seq", peer))
        around[-1].start()
    low = [pass_on("bz", 1)]
    fan(0)
    b["weight_a"][z, block] = weight_ref[:, : WIDTH // 2]
    b["weight_b"][z, block] = weight_ref[:, WIDTH // 2 :]
    dt_col = columns_of(dt_ref[...].astype(F32)) + across(bias_ref)
    dt_col = jnp.maximum(dt_col, 0.0) + jnp.log1p(jnp.exp(-jnp.abs(dt_col)))
    log_col = -jnp.exp(across(log_ref)) * dt_col
    log_high = log_col.astype(BF)
    log_low = (log_col - log_high.astype(F32)).astype(BF)
    cumul = dot(tri, log_high) + dot(tri, log_low)
    runs = dot(tri, flag_col.astype(BF))
    runs_row = dot(starts.astype(BF), tri, 1, 1)
    growth = jnp.exp(cumul)
    b["enter"][...] = split_lanes(growth, 1)
    inverse = split_lanes(jnp.exp(-cumul) * dt_col, 1)
    low_index = iota((N, WIDTH), 0)
    spread = (low_index < 2 * HG) & ((low_index & (HG - 1)) == (iota((N, WIDTH), 1) >> 6))
    b["spread"][...] = jnp.where(spread, 1.0, 0.0).astype(BF)
    skip = jnp.broadcast_to(across(skip_ref), (8, N))
    skip_high = split_lanes(skip, 1)
    skip_low = jnp.where(iota((8, N), 1) < HG, skip - two_terms(skip), 0.0).astype(BF)
    b["skip"][...] = dot(skip_high, b["spread"][...]) + dot(skip_low, b["spread"][...])

    arrived(low[0])
    low.append(pass_on("bz", 2))
    fan(1)
    fan(7)
    for one in halo:
        one.wait()
    real = jnp.where(place > 0, 1.0, 0.0)
    b["ext"][:RIM] = b["halo"][...].astype(F32) * real
    b["ext"][RIM:] = xbc_ref[...].astype(F32)
    b["flags"][:RIM] = columns_of(b["halo_starts"][...])[N - RIM :] * real
    b["flags"][RIM:] = flag_col
    crossed = b["flags"][RIM:]
    for lag in range(1, 4):
        b["keep"][lag - 1] = jnp.where(crossed == 0.0, 1.0, 0.0)
        crossed = crossed + b["flags"][RIM - lag : RIM - lag + TOK]

    def conv(c, carry):
        lanes = pl.ds(pl.multiple_of(c * N, N), N)
        acc = shift_ref[lanes][None, :] + taps_ref[3:4, lanes] * b["ext"][RIM:, lanes]
        for lag in range(1, 4):
            early = b["ext"][pl.ds(RIM - lag, TOK), lanes]
            acc = acc + taps_ref[3 - lag : 4 - lag, lanes] * early * b["keep"][lag - 1]
        b["unit"][:, lanes] = (acc / (1.0 + jnp.exp(-acc))).astype(BF)
        return carry

    lax.fori_loop(0, GW // N, conv, 0)
    for one in around:
        one.wait()
    high = [pass_on("az", 1)]

    for c in range(WIDTH // N):
        lanes = slice(c * N, (c + 1) * N)
        factor = dot(inverse, b["spread"][:, lanes])
        b["scaled"][:, lanes] = (b["unit"][:, lanes].astype(F32) * factor).astype(BF)
    bmat = b["unit"][:, WIDTH : WIDTH + N]
    cmat = b["unit"][:, WIDTH + N :]
    last = runs[TOK - 1 : TOK, :]
    tail_b = jnp.where(runs == last, bmat.astype(F32), 0.0).astype(BF)
    state = dot(b["scaled"][...], tail_b, 0, 0)
    ends = jnp.broadcast_to(growth[TOK - 1 : TOK, :], (N, N)).T
    ends = dot(b["spread"][...], split_lanes(ends, 0), 0, 0)
    state = state * ends
    unbroken = jnp.where(last == 0.0, 1.0, 0.0)
    for head in range(HG):
        at = head * P_SIZE
        b["mine"][head // 2, head % 2, :P_SIZE] = state[at : at + P_SIZE].astype(BF)
        b["mine"][head // 2, head % 2, P_SIZE:] = decay_rows(ends[at : at + 8] * unbroken)
    copies = []
    for k in range(1, ROW):
        to = (j + k) % ROW
        copies.append(copy(b["mine"].at[to], b["row"].at[j], "rows", k - 1, "seq", row_peers[k - 1]))
        copies[-1].start()
    b["row"][j] = b["mine"][j]
    scores = dot(cmat, bmat, 1, 1)
    same = lower & (jnp.concatenate([runs] * 3, axis=1) == runs_row[0:1])
    scores = jnp.where(same, scores, 0.0).astype(BF)
    b["masked_c"][...] = jnp.where(runs == 0.0, cmat.astype(F32), 0.0).astype(BF)
    for c in range(4):
        lanes = slice(c * COLS, (c + 1) * COLS)
        b["linear"][:, lanes] = dot(scores, b["scaled"][:, lanes])
    arrived(low[1])
    low.append(pass_on("bz", 3))
    for one in copies:
        one.wait()

    for head in range(2):
        total = b["row"][0, head, :P_SIZE].astype(F32)
        decay = decay_of(b["row"][0, head, P_SIZE:])
        for i in range(1, ROW):
            one = decay_of(b["row"][i, head, P_SIZE:])
            total = total * one + b["row"][i, head, :P_SIZE].astype(F32)
            decay = decay * one
        b["total"][head, :P_SIZE] = total.astype(BF)
        b["total"][head, P_SIZE:] = decay_rows(jnp.broadcast_to(decay, (8, N)))
    copies = []
    for k, peer in enumerate(column_peers):
        copies.append(copy(b["total"], b["column"].at[z], "columns", k, "seq", peer))
        copies[-1].start()
    b["column"][z] = b["total"][...]
    fan(2)
    fan(6)
    arrived(low[2])
    low.append(pass_on("bz", 4))
    fan(3)
    fan(5)
    arrived(high[0])
    high.append(pass_on("az", 2))
    for one in copies:
        one.wait()
    for head in range(2):
        state = jnp.zeros((P_SIZE, N), F32)
        for i in range(ROW - 1):
            one = decay_of(b["column"][i, head, P_SIZE:])
            later = state * one + b["column"][i, head, :P_SIZE].astype(F32)
            state = jnp.where(i < z, later, state)
        for i in range(ROW):
            b["back"][i, head] = state.astype(BF)
            if i < ROW - 1:
                one = decay_of(b["row"][i, head, P_SIZE:])
                state = state * one + b["row"][i, head, :P_SIZE].astype(F32)
    copies = []
    for k in range(1, ROW):
        to = (j + k) % ROW
        copies.append(copy(b["back"].at[to], b["land"].at[j], "backs", k - 1, "seq", row_peers[k - 1]))
        copies[-1].start()
    b["land"][j] = b["back"][j]
    arrived(low[3])
    fan(4)
    arrived(high[1])
    high.append(pass_on("az", 3))
    for one in copies:
        one.wait()

    arrived(high[2])
    high.append(pass_on("az", 4))
    square = jnp.zeros((TOK, N), F32)
    for c in range(WIDTH // N):
        lanes = slice(c * N, (c + 1) * N)
        state = b["land"][c].reshape(N, N)
        y = b["linear"][:, lanes] + dot(b["masked_c"][...], state, 1, 1)
        y = y * dot(b["enter"][...], b["spread"][:, lanes])
        y = y + b["skip"][0:1, lanes] * b["unit"][:, lanes].astype(F32)
        gate = gate_ref[:, lanes].astype(F32)
        gated = y * (gate / (1.0 + jnp.exp(-gate)))
        square = square + gated * gated
        b["gained"][:, lanes] = (gated * gain_ref[:, lanes]).astype(BF)
    square = jnp.sum(square.T, axis=0, keepdims=True)
    b["square"][...] = jnp.concatenate(
        [square[:, i * N : (i + 1) * N] for i in range(3)] + [jnp.zeros((5, N), F32)], axis=0
    )

    swap = copy(b["gained"], b["other"], "swap", 0, "seq", partner)
    swap.start()
    squares = []
    for k, peer in enumerate(head_peers):
        squares.append(copy(b["square"], b["squares"].at[h], "square", k, "head", peer))
        squares[-1].start()
    b["squares"][h] = b["square"][...]
    arrived(high[3])
    arrived(sideways)
    tokens = (b["gained"], b["other"])

    def prepare(step, side):
        for way in range(2):
            chunk = (h + 2 * HEADS - 1 - step) % HEADS if way == 0 else (h + 1 + step) % HEADS
            rows = slice(way * HALF, (way + 1) * HALF)
            term = dot(tokens[side][rows, : WIDTH // 2], b["weight_a"][chunk], 1, 1)
            term = term + dot(tokens[side][rows, WIDTH // 2 :], b["weight_b"][chunk], 1, 1)
            b["terms"][way, side] = term

    def hop(step, way, side, piece):
        at = (step, way, side, piece)
        return copy(b["send"].at[at], b["recv"].at[at], "ring", at, "head", ways[way])

    def term_of(way, side, piece):
        return b["terms"][way, side, piece * PIECE : (piece + 1) * PIECE, :]

    def summed(step, way, side, piece):
        hop(step - 1, way, side, piece).wait_recv()
        return term_of(way, side, piece) + b["recv"][step - 1, way, side, piece].astype(F32)

    places = [(side, piece, way) for side in range(2) for piece in range(2) for way in range(2)]
    prepare(0, 0)
    for side, piece, way in places:
        if (side, piece, way) == (1, 0, 0):
            swap.wait()
            prepare(0, 1)
        b["send"][0, way, side, piece] = term_of(way, side, piece).astype(BF)
        hop(0, way, side, piece).start()

    def one_step(step, carry):
        prepare(step, 0)
        prepare(step, 1)
        for side, piece, way in places:
            b["send"][step, way, side, piece] = summed(step, way, side, piece).astype(BF)
            hop(step, way, side, piece).start()
        return carry

    lax.fori_loop(1, HEADS - 1, one_step, 0)
    final = HEADS - 1
    prepare(final, 0)
    prepare(final, 1)
    homes = []
    for side, piece, way in places:
        start = way * HALF + piece * PIECE
        value = summed(final, way, side, piece)
        if side == 0:
            b["own"][start : start + PIECE, :] = value
            continue
        rows = pl.ds(start, PIECE)
        b["home"][start : start + PIECE, :] = value.astype(BF)
        at = 2 * way + piece
        homes.append(copy(b["home"].at[rows], b["home_land"].at[rows], "home", at, "seq", partner))
        homes[-1].start()
    for one in squares:
        one.wait()
    total = b["squares"][0]
    for k in range(1, HEADS):
        total = total + b["squares"][k]
    scale = columns_of(lax.rsqrt(total / DI + 1e-05))
    for one in homes:
        one.wait()
    for part in range(3):
        rows = slice(part * N, (part + 1) * N)
        factor = jnp.broadcast_to(scale[:, part : part + 1], (N, N))
        own = b["own"][rows, :]
        other = b["home_land"][rows, :].astype(F32)
        for i in range(4):
            mine = own[:, i * 64 : (i + 1) * 64]
            theirs = other[:, i * 64 : (i + 1) * 64]
            block = jnp.where(
                core == 0,
                jnp.concatenate([mine, theirs], axis=1),
                jnp.concatenate([theirs, mine], axis=1),
            )
            out_ref[rows, i * N : (i + 1) * N] = (block * factor).astype(BF)

    def drain(step, carry):
        for side, piece, way in places:
            hop(step, way, side, piece).wait_send()
        return carry

    lax.fori_loop(0, HEADS - 1, drain, 0)
    for one in sum(low + high, sideways):
        one.wait_send()


def body(
    xbc,
    gate_z,
    dt_raw,
    dt_bias,
    a_log,
    skip_d,
    conv_weight,
    conv_bias,
    norm_gain,
    out_weight,
    starts,
):
    sems = [pltpu.SemaphoreType.DMA(shape) for shape in SEMS.values()]
    return pl.pallas_call(
        layer_kernel,
        out_shape=jax.ShapeDtypeStruct((TOK, 2 * COLS), BF),
        in_specs=[pl.BlockSpec(memory_space=pltpu.VMEM)] * 11,
        out_specs=pl.BlockSpec(memory_space=pltpu.VMEM),
        scratch_shapes=[pltpu.VMEM(*spec) for spec in SHAPES.values()] + sems + sems,
        compiler_params=pltpu.CompilerParams(collective_id=0, has_side_effects=True),
        name="layer",
    )(
        xbc, gate_z, dt_raw, dt_bias[None, :], a_log[None, :], skip_d[None, :], conv_weight,
        conv_bias, norm_gain[None, :], out_weight.T, starts,
    )


def solution(mesh):
    placed = (
        P("seq", "head"),
        P("seq", "head"),
        P("head", "seq"),
        P("head"),
        P("head"),
        P("head"),
        P(None, "head"),
        P("head"),
        P("head"),
        P("head", "seq"),
        P("seq"),
    )
    return jax.shard_map(
        body, mesh=mesh, in_specs=placed, out_specs=P("seq", "head"), check_vma=False
    )
```

```python
import jax
import jax.numpy as jnp
from jax import lax
from jax.experimental import pallas as pl
from jax.experimental.pallas import tpu as pltpu
from jax.sharding import PartitionSpec as P

MESH = pl.DeviceIdType.MESH
P_SIZE = 64
N = 128
DI = 8192
HG = 16
GW = 1280
TOK = 384
RIM = 16
WIDTH = HG * P_SIZE
PART = P_SIZE + 16
ROW = 8
HEADS = 8
HALF = 192
PIECE = 96
COLS = 256
BF = jnp.bfloat16
F32 = jnp.float32
SHAPES = dict(
    halo=((RIM, GW), BF),
    halo_starts=((8, N), F32),
    starts=((8, TOK), F32),
    skip=((8, WIDTH), F32),
    ext=((RIM + TOK, GW), F32),
    flags=((RIM + TOK, N), F32),
    keep=((3, TOK, N), F32),
    unit=((TOK, GW), BF),
    spread=((N, WIDTH), BF),
    scaled=((TOK, WIDTH), BF),
    linear=((TOK, WIDTH), F32),
    enter=((TOK, N), BF),
    masked_c=((TOK, N), BF),
    mine=((ROW, 2, PART, N), BF),
    row=((ROW, 2, PART, N), BF),
    total=((2, PART, N), BF),
    column=((ROW, 2, PART, N), BF),
    back=((ROW, 2, P_SIZE, N), BF),
    land=((ROW, 2, P_SIZE, N), BF),
    weight_a=((HEADS, COLS, WIDTH // 2), BF),
    weight_b=((HEADS, COLS, WIDTH // 2), BF),
    gained=((TOK, WIDTH), BF),
    other=((TOK, WIDTH), BF),
    send=((HEADS - 1, 2, 2, 2, PIECE, COLS), BF),
    recv=((HEADS - 1, 2, 2, 2, PIECE, COLS), BF),
    terms=((2, 2, HALF, COLS), F32),
    square=((8, N), F32),
    squares=((HEADS, 8, N), F32),
    own=((TOK, COLS), F32),
    home=((TOK, COLS), BF),
    home_land=((TOK, COLS), BF),
)
SEMS = dict(
    halo=(2,), ax=(3,), az=(4, 2), bz=(4, 2), bx=(ROW, 4), rows=(7,), columns=(7,), backs=(7,),
    swap=(1,), ring=(HEADS - 1, 2, 2, 2), square=(7,), home=(4,),
)


def dot(a, b, ca=1, cb=0):
    return lax.dot_general(a, b, (((ca,), (cb,)), ((), ())), preferred_element_type=F32)


def iota(shape, axis):
    return lax.broadcasted_iota(jnp.int32, shape, axis)


def split_lanes(value, axis):
    high = value.astype(BF).astype(F32)
    index = iota(value.shape, axis)
    pair = jnp.where(index < HG, high, jnp.where(index < 2 * HG, value - high, 0.0))
    return pair.astype(BF)


def decay_of(tile):
    both = tile.astype(F32)
    return both[0:1] + both[8:9]


def decay_rows(decay):
    high = decay.astype(BF).astype(F32)
    return jnp.concatenate([high, decay - high], axis=0).astype(BF)


def two_terms(value):
    high = value.astype(BF).astype(F32)
    return high + (value - high).astype(BF).astype(F32)


def across(ref):
    return jnp.concatenate([ref[...]] * (N // HG), axis=1)


def columns_of(rows):
    return jnp.concatenate([rows] * (N // rows.shape[0]), axis=0).T


def layer_kernel(
    xbc_ref, gate_ref, dt_ref, bias_ref, log_ref, skip_ref, taps_ref, shift_ref, gain_ref,
    weight_ref, starts_ref, out_ref, *scratch,
):
    names = list(SHAPES)
    b = dict(zip(names, scratch[: len(names)]))
    sems = scratch[len(names) :]
    ss = dict(zip(SEMS, sems[: len(SEMS)]))
    rs = dict(zip(SEMS, sems[len(SEMS) :]))
    place = lax.axis_index("seq")
    h = lax.axis_index("head")
    z = place // ROW
    j = place % ROW
    x = j // 2
    core = j % 2
    partner = place + 1 - 2 * core
    after = (place + 1) % 64
    before = (place + 63) % 64
    row_peers = [z * ROW + (j + k) % ROW for k in range(1, ROW)]
    column_peers = [((z + k) % ROW) * ROW + j for k in range(1, ROW)]
    head_peers = [(h + k) % HEADS for k in range(1, HEADS)]
    ways = (head_peers[0], head_peers[-1])

    barrier = pltpu.get_barrier_semaphore()
    for peer in row_peers + column_peers + [after, before]:
        pl.semaphore_signal(barrier, 1, device_id={"seq": peer}, device_id_type=MESH)
    for peer in head_peers:
        pl.semaphore_signal(barrier, 1, device_id={"head": peer}, device_id_type=MESH)

    def copy(src, dst, name, at, axis, peer):
        return pltpu.make_async_remote_copy(
            src, dst, ss[name].at[at], rs[name].at[at],
            device_id={axis: peer}, device_id_type=MESH,
        )

    block = pl.ds(pl.multiple_of(x * 64, 64), 64)
    halves = (pl.ds(0, WIDTH // 2), pl.ds(WIDTH // 2, WIDTH // 2))
    side_peers = [z * ROW + ((x + k) % 4) * 2 + core for k in range(1, 4)]

    near = {}
    far = []

    def fan(turn):
        chunk = (z + turn) % ROW
        part = b["weight_b"].at[chunk, block]
        source = weight_ref.at[:, halves[1]] if turn == 0 else part
        near[turn] = [
            copy(source, part, "bx", (turn, way), "seq", peer)
            for way, peer in enumerate((side_peers[0], side_peers[2]))
        ]
        for one in near[turn]:
            one.start()

    def relay(turn):
        chunk = (z + turn) % ROW
        arrived(near[turn])
        for way, peer in enumerate((side_peers[0], side_peers[2])):
            source_x = (x + 3) % 4 if way == 0 else (x + 1) % 4
            rows = pl.ds(pl.multiple_of(source_x * 64 + way * 32, 32), 32)
            part = b["weight_b"].at[chunk, rows]
            far.append(copy(part, part, "bx", (turn, 2 + way), "seq", peer))
            far[-1].start()

    def pass_on(name, step):
        pair = []
        for way, peer in enumerate((column_peers[0], column_peers[-1])):
            chunk = (z + 9 - step) % ROW if way == 0 else (z + step - 1) % ROW
            first, count = (0, COLS) if name == "az" else (x * 64, 64)
            if step == 4:
                count = count // 2
                first = first + way * count
            rows = pl.ds(pl.multiple_of(first, count), count)
            part = b["weight_a" if name == "az" else "weight_b"].at[chunk, rows]
            source = part
            if name == "bz" and step == 1:
                source = weight_ref.at[:, halves[1]]
            pair.append(copy(source, part, name, (step - 1, way), "seq", peer))
            pair[-1].start()
        return pair

    def arrived(pair):
        for one in pair:
            one.wait_recv()

    starts = jnp.broadcast_to(starts_ref[...].astype(F32)[None, :], (8, TOK))
    b["starts"][...] = starts
    lower = iota((TOK, TOK), 0) >= iota((TOK, TOK), 1)
    tri = jnp.where(lower, 1.0, 0.0).astype(BF)
    flag_col = columns_of(starts)
    pl.semaphore_wait(barrier, 23)
    halo = [
        copy(xbc_ref.at[pl.ds(TOK - RIM, RIM)], b["halo"], "halo", 0, "seq", after),
        copy(
            b["starts"].at[:, pl.ds(TOK - N, N)], b["halo_starts"], "halo", 1, "seq", after
        ),
    ]
    for one in halo:
        one.start()
    around = []
    for k, peer in enumerate(side_peers):
        part = b["weight_a"].at[z, block]
        around.append(copy(weight_ref.at[:, halves[0]], part, "ax", k, "seq", peer))
        around[-1].start()
    low = [pass_on("bz", 1)]
    fan(0)
    b["weight_a"][z, block] = weight_ref[:, : WIDTH // 2]
    b["weight_b"][z, block] = weight_ref[:, WIDTH // 2 :]
    dt_col = columns_of(dt_ref[...].astype(F32)) + across(bias_ref)
    dt_col = jnp.maximum(dt_col, 0.0) + jnp.log1p(jnp.exp(-jnp.abs(dt_col)))
    log_col = -jnp.exp(across(log_ref)) * dt_col
    log_high = log_col.astype(BF)
    log_low = (log_col - log_high.astype(F32)).astype(BF)
    cumul = dot(tri, log_high) + dot(tri, log_low)
    runs = dot(tri, flag_col.astype(BF))
    runs_row = dot(starts.astype(BF), tri, 1, 1)
    growth = jnp.exp(cumul)
    b["enter"][...] = split_lanes(growth, 1)
    inverse = split_lanes(jnp.exp(-cumul) * dt_col, 1)
    low_index = iota((N, WIDTH), 0)
    spread = (low_index < 2 * HG) & ((low_index & (HG - 1)) == (iota((N, WIDTH), 1) >> 6))
    b["spread"][...] = jnp.where(spread, 1.0, 0.0).astype(BF)
    skip = jnp.broadcast_to(across(skip_ref), (8, N))
    skip_high = split_lanes(skip, 1)
    skip_low = jnp.where(iota((8, N), 1) < HG, skip - two_terms(skip), 0.0).astype(BF)
    b["skip"][...] = dot(skip_high, b["spread"][...]) + dot(skip_low, b["spread"][...])

    arrived(low[0])
    low.append(pass_on("bz", 2))
    fan(1)
    fan(7)
    relay(0)
    for one in halo:
        one.wait()
    real = jnp.where(place > 0, 1.0, 0.0)
    b["ext"][:RIM] = b["halo"][...].astype(F32) * real
    b["ext"][RIM:] = xbc_ref[...].astype(F32)
    b["flags"][:RIM] = columns_of(b["halo_starts"][...])[N - RIM :] * real
    b["flags"][RIM:] = flag_col
    crossed = b["flags"][RIM:]
    for lag in range(1, 4):
        b["keep"][lag - 1] = jnp.where(crossed == 0.0, 1.0, 0.0)
        crossed = crossed + b["flags"][RIM - lag : RIM - lag + TOK]

    def conv(c, carry):
        lanes = pl.ds(pl.multiple_of(c * N, N), N)
        acc = shift_ref[lanes][None, :] + taps_ref[3:4, lanes] * b["ext"][RIM:, lanes]
        for lag in range(1, 4):
            early = b["ext"][pl.ds(RIM - lag, TOK), lanes]
            acc = acc + taps_ref[3 - lag : 4 - lag, lanes] * early * b["keep"][lag - 1]
        b["unit"][:, lanes] = (acc / (1.0 + jnp.exp(-acc))).astype(BF)
        return carry

    lax.fori_loop(0, GW // N, conv, 0)
    for one in around:
        one.wait()
    high = [pass_on("az", 1)]

    for c in range(WIDTH // N):
        lanes = slice(c * N, (c + 1) * N)
        factor = dot(inverse, b["spread"][:, lanes])
        b["scaled"][:, lanes] = (b["unit"][:, lanes].astype(F32) * factor).astype(BF)
    bmat = b["unit"][:, WIDTH : WIDTH + N]
    cmat = b["unit"][:, WIDTH + N :]
    last = runs[TOK - 1 : TOK, :]
    tail_b = jnp.where(runs == last, bmat.astype(F32), 0.0).astype(BF)
    state = dot(b["scaled"][...], tail_b, 0, 0)
    ends = jnp.broadcast_to(growth[TOK - 1 : TOK, :], (N, N)).T
    ends = dot(b["spread"][...], split_lanes(ends, 0), 0, 0)
    state = state * ends
    unbroken = jnp.where(last == 0.0, 1.0, 0.0)
    for head in range(HG):
        at = head * P_SIZE
        b["mine"][head // 2, head % 2, :P_SIZE] = state[at : at + P_SIZE].astype(BF)
        b["mine"][head // 2, head % 2, P_SIZE:] = decay_rows(ends[at : at + 8] * unbroken)
    copies = []
    for k in range(1, ROW):
        to = (j + k) % ROW
        copies.append(copy(b["mine"].at[to], b["row"].at[j], "rows", k - 1, "seq", row_peers[k - 1]))
        copies[-1].start()
    b["row"][j] = b["mine"][j]
    scores = dot(cmat, bmat, 1, 1)
    same = lower & (jnp.concatenate([runs] * 3, axis=1) == runs_row[0:1])
    scores = jnp.where(same, scores, 0.0).astype(BF)
    b["masked_c"][...] = jnp.where(runs == 0.0, cmat.astype(F32), 0.0).astype(BF)
    for c in range(4):
        lanes = slice(c * COLS, (c + 1) * COLS)
        b["linear"][:, lanes] = dot(scores, b["scaled"][:, lanes])
    arrived(low[1])
    low.append(pass_on("bz", 3))
    for one in copies:
        one.wait()

    for head in range(2):
        total = b["row"][0, head, :P_SIZE].astype(F32)
        decay = decay_of(b["row"][0, head, P_SIZE:])
        for i in range(1, ROW):
            one = decay_of(b["row"][i, head, P_SIZE:])
            total = total * one + b["row"][i, head, :P_SIZE].astype(F32)
            decay = decay * one
        b["total"][head, :P_SIZE] = total.astype(BF)
        b["total"][head, P_SIZE:] = decay_rows(jnp.broadcast_to(decay, (8, N)))
    copies = []
    for k, peer in enumerate(column_peers):
        copies.append(copy(b["total"], b["column"].at[z], "columns", k, "seq", peer))
        copies[-1].start()
    b["column"][z] = b["total"][...]
    fan(2)
    fan(6)
    relay(1)
    relay(7)
    arrived(low[2])
    low.append(pass_on("bz", 4))
    fan(3)
    fan(5)
    arrived(high[0])
    high.append(pass_on("az", 2))
    for one in copies:
        one.wait()
    for head in range(2):
        state = jnp.zeros((P_SIZE, N), F32)
        for i in range(ROW - 1):
            one = decay_of(b["column"][i, head, P_SIZE:])
            later = state * one + b["column"][i, head, :P_SIZE].astype(F32)
            state = jnp.where(i < z, later, state)
        for i in range(ROW):
            b["back"][i, head] = state.astype(BF)
            if i < ROW - 1:
                one = decay_of(b["row"][i, head, P_SIZE:])
                state = state * one + b["row"][i, head, :P_SIZE].astype(F32)
    copies = []
    for k in range(1, ROW):
        to = (j + k) % ROW
        copies.append(copy(b["back"].at[to], b["land"].at[j], "backs", k - 1, "seq", row_peers[k - 1]))
        copies[-1].start()
    b["land"][j] = b["back"][j]
    arrived(low[3])
    fan(4)
    for turn in (2, 6, 3, 5):
        relay(turn)
    arrived(high[1])
    high.append(pass_on("az", 3))
    for one in copies:
        one.wait()

    arrived(high[2])
    high.append(pass_on("az", 4))
    square = jnp.zeros((TOK, N), F32)
    for c in range(WIDTH // N):
        lanes = slice(c * N, (c + 1) * N)
        state = b["land"][c].reshape(N, N)
        y = b["linear"][:, lanes] + dot(b["masked_c"][...], state, 1, 1)
        y = y * dot(b["enter"][...], b["spread"][:, lanes])
        y = y + b["skip"][0:1, lanes] * b["unit"][:, lanes].astype(F32)
        gate = gate_ref[:, lanes].astype(F32)
        gated = y * (gate / (1.0 + jnp.exp(-gate)))
        square = square + gated * gated
        b["gained"][:, lanes] = (gated * gain_ref[:, lanes]).astype(BF)
    square = jnp.sum(square.T, axis=0, keepdims=True)
    b["square"][...] = jnp.concatenate(
        [square[:, i * N : (i + 1) * N] for i in range(3)] + [jnp.zeros((5, N), F32)], axis=0
    )

    swap = copy(b["gained"], b["other"], "swap", 0, "seq", partner)
    swap.start()
    squares = []
    for k, peer in enumerate(head_peers):
        squares.append(copy(b["square"], b["squares"].at[h], "square", k, "head", peer))
        squares[-1].start()
    b["squares"][h] = b["square"][...]
    relay(4)
    arrived(high[3])
    arrived(far)
    tokens = (b["gained"], b["other"])

    def prepare(step, side):
        for way in range(2):
            chunk = (h + 2 * HEADS - 1 - step) % HEADS if way == 0 else (h + 1 + step) % HEADS
            rows = slice(way * HALF, (way + 1) * HALF)
            term = dot(tokens[side][rows, : WIDTH // 2], b["weight_a"][chunk], 1, 1)
            term = term + dot(tokens[side][rows, WIDTH // 2 :], b["weight_b"][chunk], 1, 1)
            b["terms"][way, side] = term

    def hop(step, way, side, piece):
        at = (step, way, side, piece)
        return copy(b["send"].at[at], b["recv"].at[at], "ring", at, "head", ways[way])

    def term_of(way, side, piece):
        return b["terms"][way, side, piece * PIECE : (piece + 1) * PIECE, :]

    def summed(step, way, side, piece):
        hop(step - 1, way, side, piece).wait_recv()
        return term_of(way, side, piece) + b["recv"][step - 1, way, side, piece].astype(F32)

    places = [(side, piece, way) for side in range(2) for piece in range(2) for way in range(2)]
    prepare(0, 0)
    for side, piece, way in places:
        if (side, piece, way) == (1, 0, 0):
            swap.wait()
            prepare(0, 1)
        b["send"][0, way, side, piece] = term_of(way, side, piece).astype(BF)
        hop(0, way, side, piece).start()

    def one_step(step, carry):
        prepare(step, 0)
        prepare(step, 1)
        for side, piece, way in places:
            b["send"][step, way, side, piece] = summed(step, way, side, piece).astype(BF)
            hop(step, way, side, piece).start()
        return carry

    lax.fori_loop(1, HEADS - 1, one_step, 0)
    final = HEADS - 1
    prepare(final, 0)
    prepare(final, 1)
    homes = []
    for side, piece, way in places:
        start = way * HALF + piece * PIECE
        value = summed(final, way, side, piece)
        if side == 0:
            b["own"][start : start + PIECE, :] = value
            continue
        rows = pl.ds(start, PIECE)
        b["home"][start : start + PIECE, :] = value.astype(BF)
        at = 2 * way + piece
        homes.append(copy(b["home"].at[rows], b["home_land"].at[rows], "home", at, "seq", partner))
        homes[-1].start()
    for one in squares:
        one.wait()
    total = b["squares"][0]
    for k in range(1, HEADS):
        total = total + b["squares"][k]
    scale = columns_of(lax.rsqrt(total / DI + 1e-05))
    for one in homes:
        one.wait()
    for part in range(3):
        rows = slice(part * N, (part + 1) * N)
        factor = jnp.broadcast_to(scale[:, part : part + 1], (N, N))
        own = b["own"][rows, :]
        other = b["home_land"][rows, :].astype(F32)
        for i in range(4):
            mine = own[:, i * 64 : (i + 1) * 64]
            theirs = other[:, i * 64 : (i + 1) * 64]
            block = jnp.where(
                core == 0,
                jnp.concatenate([mine, theirs], axis=1),
                jnp.concatenate([theirs, mine], axis=1),
            )
            out_ref[rows, i * N : (i + 1) * N] = (block * factor).astype(BF)

    def drain(step, carry):
        for side, piece, way in places:
            hop(step, way, side, piece).wait_send()
        return carry

    lax.fori_loop(0, HEADS - 1, drain, 0)
    for one in sum(low + high + list(near.values()), far):
        one.wait_send()


def body(
    xbc,
    gate_z,
    dt_raw,
    dt_bias,
    a_log,
    skip_d,
    conv_weight,
    conv_bias,
    norm_gain,
    out_weight,
    starts,
):
    sems = [pltpu.SemaphoreType.DMA(shape) for shape in SEMS.values()]
    return pl.pallas_call(
        layer_kernel,
        out_shape=jax.ShapeDtypeStruct((TOK, 2 * COLS), BF),
        in_specs=[pl.BlockSpec(memory_space=pltpu.VMEM)] * 11,
        out_specs=pl.BlockSpec(memory_space=pltpu.VMEM),
        scratch_shapes=[pltpu.VMEM(*spec) for spec in SHAPES.values()] + sems + sems,
        compiler_params=pltpu.CompilerParams(collective_id=0, has_side_effects=True),
        name="layer",
    )(
        xbc, gate_z, dt_raw, dt_bias[None, :], a_log[None, :], skip_d[None, :], conv_weight,
        conv_bias, norm_gain[None, :], out_weight.T, starts,
    )


def solution(mesh):
    placed = (
        P("seq", "head"),
        P("seq", "head"),
        P("head", "seq"),
        P("head"),
        P("head"),
        P("head"),
        P(None, "head"),
        P("head"),
        P("head"),
        P("head", "seq"),
        P("seq"),
    )
    return jax.shard_map(
        body, mesh=mesh, in_specs=placed, out_specs=P("seq", "head"), check_vma=False
    )
```

```python
import jax
import jax.numpy as jnp
from jax import lax
from jax.experimental import pallas as pl
from jax.experimental.pallas import tpu as pltpu
from jax.sharding import PartitionSpec as P

MESH = pl.DeviceIdType.MESH
P_SIZE = 64
N = 128
DI = 8192
HG = 16
GW = 1280
TOK = 384
RIM = 16
WIDTH = HG * P_SIZE
SPLIT = 384
PART = P_SIZE + 16
ROW = 8
HEADS = 8
HALF = 192
PIECE = 96
COLS = 256
BF = jnp.bfloat16
F32 = jnp.float32
SHAPES = dict(
    halo=((RIM, GW), BF),
    halo_starts=((8, N), F32),
    starts=((8, TOK), F32),
    skip=((8, WIDTH), F32),
    ext=((RIM + TOK, GW), F32),
    flags=((RIM + TOK, N), F32),
    keep=((3, TOK, N), F32),
    unit=((TOK, GW), BF),
    spread=((N, WIDTH), BF),
    scaled=((TOK, WIDTH), BF),
    linear=((TOK, WIDTH), F32),
    enter=((TOK, N), BF),
    masked_c=((TOK, N), BF),
    mine=((ROW, 2, PART, N), BF),
    row=((ROW, 2, PART, N), BF),
    total=((2, PART, N), BF),
    column=((ROW, 2, PART, N), BF),
    back=((ROW, 2, P_SIZE, N), BF),
    land=((ROW, 2, P_SIZE, N), BF),
    weight_a=((HEADS, COLS, SPLIT), BF),
    weight_b=((HEADS, COLS, WIDTH - SPLIT), BF),
    gained=((TOK, WIDTH), BF),
    other=((TOK, WIDTH), BF),
    send=((HEADS - 1, 2, 2, 2, PIECE, COLS), BF),
    recv=((HEADS - 1, 2, 2, 2, PIECE, COLS), BF),
    terms=((2, 2, HALF, COLS), F32),
    square=((8, N), F32),
    squares=((HEADS, 8, N), F32),
    own=((TOK, COLS), F32),
    home=((TOK, COLS), BF),
    home_land=((TOK, COLS), BF),
)
SEMS = dict(
    halo=(2,), ax=(3,), az=(4, 2), bz=(4, 2), bx=(ROW, 4), rows=(7,), columns=(7,), backs=(7,),
    swap=(1,), ring=(HEADS - 1, 2, 2, 2), square=(7,), home=(4,),
)


def dot(a, b, ca=1, cb=0):
    return lax.dot_general(a, b, (((ca,), (cb,)), ((), ())), preferred_element_type=F32)


def iota(shape, axis):
    return lax.broadcasted_iota(jnp.int32, shape, axis)


def split_lanes(value, axis):
    high = value.astype(BF).astype(F32)
    index = iota(value.shape, axis)
    pair = jnp.where(index < HG, high, jnp.where(index < 2 * HG, value - high, 0.0))
    return pair.astype(BF)


def decay_of(tile):
    both = tile.astype(F32)
    return both[0:1] + both[8:9]


def decay_rows(decay):
    high = decay.astype(BF).astype(F32)
    return jnp.concatenate([high, decay - high], axis=0).astype(BF)


def two_terms(value):
    high = value.astype(BF).astype(F32)
    return high + (value - high).astype(BF).astype(F32)


def across(ref):
    return jnp.concatenate([ref[...]] * (N // HG), axis=1)


def columns_of(rows):
    return jnp.concatenate([rows] * (N // rows.shape[0]), axis=0).T


def layer_kernel(
    xbc_ref, gate_ref, dt_ref, bias_ref, log_ref, skip_ref, taps_ref, shift_ref, gain_ref,
    weight_ref, starts_ref, out_ref, *scratch,
):
    names = list(SHAPES)
    b = dict(zip(names, scratch[: len(names)]))
    sems = scratch[len(names) :]
    ss = dict(zip(SEMS, sems[: len(SEMS)]))
    rs = dict(zip(SEMS, sems[len(SEMS) :]))
    place = lax.axis_index("seq")
    h = lax.axis_index("head")
    z = place // ROW
    j = place % ROW
    x = j // 2
    core = j % 2
    partner = place + 1 - 2 * core
    after = (place + 1) % 64
    before = (place + 63) % 64
    row_peers = [z * ROW + (j + k) % ROW for k in range(1, ROW)]
    column_peers = [((z + k) % ROW) * ROW + j for k in range(1, ROW)]
    head_peers = [(h + k) % HEADS for k in range(1, HEADS)]
    ways = (head_peers[0], head_peers[-1])

    barrier = pltpu.get_barrier_semaphore()
    for peer in row_peers + column_peers + [after, before]:
        pl.semaphore_signal(barrier, 1, device_id={"seq": peer}, device_id_type=MESH)
    for peer in head_peers:
        pl.semaphore_signal(barrier, 1, device_id={"head": peer}, device_id_type=MESH)

    def copy(src, dst, name, at, axis, peer):
        return pltpu.make_async_remote_copy(
            src, dst, ss[name].at[at], rs[name].at[at],
            device_id={axis: peer}, device_id_type=MESH,
        )

    block = pl.ds(pl.multiple_of(x * 64, 64), 64)
    halves = (pl.ds(0, SPLIT), pl.ds(SPLIT, WIDTH - SPLIT))
    side_peers = [z * ROW + ((x + k) % 4) * 2 + core for k in range(1, 4)]

    near = {}
    far = []

    def fan(turn):
        chunk = (z + turn) % ROW
        part = b["weight_b"].at[chunk, block]
        source = weight_ref.at[:, halves[1]] if turn == 0 else part
        near[turn] = [
            copy(source, part, "bx", (turn, way), "seq", peer)
            for way, peer in enumerate((side_peers[0], side_peers[2]))
        ]
        for one in near[turn]:
            one.start()

    def relay(turn):
        chunk = (z + turn) % ROW
        arrived(near[turn])
        for way, peer in enumerate((side_peers[0], side_peers[2])):
            source_x = (x + 3) % 4 if way == 0 else (x + 1) % 4
            rows = pl.ds(pl.multiple_of(source_x * 64 + way * 32, 32), 32)
            part = b["weight_b"].at[chunk, rows]
            far.append(copy(part, part, "bx", (turn, 2 + way), "seq", peer))
            far[-1].start()

    def pass_on(name, step):
        pair = []
        for way, peer in enumerate((column_peers[0], column_peers[-1])):
            chunk = (z + 9 - step) % ROW if way == 0 else (z + step - 1) % ROW
            first, count = (0, COLS) if name == "az" else (x * 64, 64)
            if step == 4:
                count = count // 2
                first = first + way * count
            rows = pl.ds(pl.multiple_of(first, count), count)
            part = b["weight_a" if name == "az" else "weight_b"].at[chunk, rows]
            source = part
            if name == "bz" and step == 1:
                source = weight_ref.at[:, halves[1]]
            pair.append(copy(source, part, name, (step - 1, way), "seq", peer))
            pair[-1].start()
        return pair

    def arrived(pair):
        for one in pair:
            one.wait_recv()

    starts = jnp.broadcast_to(starts_ref[...].astype(F32)[None, :], (8, TOK))
    b["starts"][...] = starts
    lower = iota((TOK, TOK), 0) >= iota((TOK, TOK), 1)
    tri = jnp.where(lower, 1.0, 0.0).astype(BF)
    flag_col = columns_of(starts)
    pl.semaphore_wait(barrier, 23)
    halo = [
        copy(xbc_ref.at[pl.ds(TOK - RIM, RIM)], b["halo"], "halo", 0, "seq", after),
        copy(
            b["starts"].at[:, pl.ds(TOK - N, N)], b["halo_starts"], "halo", 1, "seq", after
        ),
    ]
    for one in halo:
        one.start()
    around = []
    for k, peer in enumerate(side_peers):
        part = b["weight_a"].at[z, block]
        around.append(copy(weight_ref.at[:, halves[0]], part, "ax", k, "seq", peer))
        around[-1].start()
    low = [pass_on("bz", 1)]
    fan(0)
    b["weight_a"][z, block] = weight_ref[:, : SPLIT]
    b["weight_b"][z, block] = weight_ref[:, SPLIT:]
    dt_col = columns_of(dt_ref[...].astype(F32)) + across(bias_ref)
    dt_col = jnp.maximum(dt_col, 0.0) + jnp.log1p(jnp.exp(-jnp.abs(dt_col)))
    log_col = -jnp.exp(across(log_ref)) * dt_col
    log_high = log_col.astype(BF)
    log_low = (log_col - log_high.astype(F32)).astype(BF)
    cumul = dot(tri, log_high) + dot(tri, log_low)
    runs = dot(tri, flag_col.astype(BF))
    runs_row = dot(starts.astype(BF), tri, 1, 1)
    growth = jnp.exp(cumul)
    b["enter"][...] = split_lanes(growth, 1)
    inverse = split_lanes(jnp.exp(-cumul) * dt_col, 1)
    low_index = iota((N, WIDTH), 0)
    spread = (low_index < 2 * HG) & ((low_index & (HG - 1)) == (iota((N, WIDTH), 1) >> 6))
    b["spread"][...] = jnp.where(spread, 1.0, 0.0).astype(BF)
    skip = jnp.broadcast_to(across(skip_ref), (8, N))
    skip_high = split_lanes(skip, 1)
    skip_low = jnp.where(iota((8, N), 1) < HG, skip - two_terms(skip), 0.0).astype(BF)
    b["skip"][...] = dot(skip_high, b["spread"][...]) + dot(skip_low, b["spread"][...])

    arrived(low[0])
    low.append(pass_on("bz", 2))
    fan(1)
    fan(7)
    relay(0)
    for one in halo:
        one.wait()
    real = jnp.where(place > 0, 1.0, 0.0)
    b["ext"][:RIM] = b["halo"][...].astype(F32) * real
    b["ext"][RIM:] = xbc_ref[...].astype(F32)
    b["flags"][:RIM] = columns_of(b["halo_starts"][...])[N - RIM :] * real
    b["flags"][RIM:] = flag_col
    crossed = b["flags"][RIM:]
    for lag in range(1, 4):
        b["keep"][lag - 1] = jnp.where(crossed == 0.0, 1.0, 0.0)
        crossed = crossed + b["flags"][RIM - lag : RIM - lag + TOK]

    def conv(c, carry):
        lanes = pl.ds(pl.multiple_of(c * N, N), N)
        acc = shift_ref[lanes][None, :] + taps_ref[3:4, lanes] * b["ext"][RIM:, lanes]
        for lag in range(1, 4):
            early = b["ext"][pl.ds(RIM - lag, TOK), lanes]
            acc = acc + taps_ref[3 - lag : 4 - lag, lanes] * early * b["keep"][lag - 1]
        b["unit"][:, lanes] = (acc / (1.0 + jnp.exp(-acc))).astype(BF)
        return carry

    lax.fori_loop(0, GW // N, conv, 0)
    for one in around:
        one.wait()
    high = [pass_on("az", 1)]

    for c in range(WIDTH // N):
        lanes = slice(c * N, (c + 1) * N)
        factor = dot(inverse, b["spread"][:, lanes])
        b["scaled"][:, lanes] = (b["unit"][:, lanes].astype(F32) * factor).astype(BF)
    bmat = b["unit"][:, WIDTH : WIDTH + N]
    cmat = b["unit"][:, WIDTH + N :]
    last = runs[TOK - 1 : TOK, :]
    tail_b = jnp.where(runs == last, bmat.astype(F32), 0.0).astype(BF)
    state = dot(b["scaled"][...], tail_b, 0, 0)
    ends = jnp.broadcast_to(growth[TOK - 1 : TOK, :], (N, N)).T
    ends = dot(b["spread"][...], split_lanes(ends, 0), 0, 0)
    state = state * ends
    unbroken = jnp.where(last == 0.0, 1.0, 0.0)
    for head in range(HG):
        at = head * P_SIZE
        b["mine"][head // 2, head % 2, :P_SIZE] = state[at : at + P_SIZE].astype(BF)
        b["mine"][head // 2, head % 2, P_SIZE:] = decay_rows(ends[at : at + 8] * unbroken)
    copies = []
    for k in range(1, ROW):
        to = (j + k) % ROW
        copies.append(copy(b["mine"].at[to], b["row"].at[j], "rows", k - 1, "seq", row_peers[k - 1]))
        copies[-1].start()
    b["row"][j] = b["mine"][j]
    scores = dot(cmat, bmat, 1, 1)
    same = lower & (jnp.concatenate([runs] * 3, axis=1) == runs_row[0:1])
    scores = jnp.where(same, scores, 0.0).astype(BF)
    b["masked_c"][...] = jnp.where(runs == 0.0, cmat.astype(F32), 0.0).astype(BF)
    for c in range(4):
        lanes = slice(c * COLS, (c + 1) * COLS)
        b["linear"][:, lanes] = dot(scores, b["scaled"][:, lanes])
    arrived(low[1])
    low.append(pass_on("bz", 3))
    for one in copies:
        one.wait()

    for head in range(2):
        total = b["row"][0, head, :P_SIZE].astype(F32)
        decay = decay_of(b["row"][0, head, P_SIZE:])
        for i in range(1, ROW):
            one = decay_of(b["row"][i, head, P_SIZE:])
            total = total * one + b["row"][i, head, :P_SIZE].astype(F32)
            decay = decay * one
        b["total"][head, :P_SIZE] = total.astype(BF)
        b["total"][head, P_SIZE:] = decay_rows(jnp.broadcast_to(decay, (8, N)))
    copies = []
    for k, peer in enumerate(column_peers):
        copies.append(copy(b["total"], b["column"].at[z], "columns", k, "seq", peer))
        copies[-1].start()
    b["column"][z] = b["total"][...]
    fan(2)
    fan(6)
    relay(1)
    relay(7)
    arrived(low[2])
    low.append(pass_on("bz", 4))
    fan(3)
    fan(5)
    arrived(high[0])
    high.append(pass_on("az", 2))
    for one in copies:
        one.wait()
    for head in range(2):
        state = jnp.zeros((P_SIZE, N), F32)
        for i in range(ROW - 1):
            one = decay_of(b["column"][i, head, P_SIZE:])
            later = state * one + b["column"][i, head, :P_SIZE].astype(F32)
            state = jnp.where(i < z, later, state)
        for i in range(ROW):
            b["back"][i, head] = state.astype(BF)
            if i < ROW - 1:
                one = decay_of(b["row"][i, head, P_SIZE:])
                state = state * one + b["row"][i, head, :P_SIZE].astype(F32)
    copies = []
    for k in range(1, ROW):
        to = (j + k) % ROW
        copies.append(copy(b["back"].at[to], b["land"].at[j], "backs", k - 1, "seq", row_peers[k - 1]))
        copies[-1].start()
    b["land"][j] = b["back"][j]
    arrived(low[3])
    fan(4)
    for turn in (2, 6, 3, 5):
        relay(turn)
    arrived(high[1])
    high.append(pass_on("az", 3))
    for one in copies:
        one.wait()

    arrived(high[2])
    high.append(pass_on("az", 4))
    square = jnp.zeros((TOK, N), F32)
    for c in range(WIDTH // N):
        lanes = slice(c * N, (c + 1) * N)
        state = b["land"][c].reshape(N, N)
        y = b["linear"][:, lanes] + dot(b["masked_c"][...], state, 1, 1)
        y = y * dot(b["enter"][...], b["spread"][:, lanes])
        y = y + b["skip"][0:1, lanes] * b["unit"][:, lanes].astype(F32)
        gate = gate_ref[:, lanes].astype(F32)
        gated = y * (gate / (1.0 + jnp.exp(-gate)))
        square = square + gated * gated
        b["gained"][:, lanes] = (gated * gain_ref[:, lanes]).astype(BF)
    square = jnp.sum(square.T, axis=0, keepdims=True)
    b["square"][...] = jnp.concatenate(
        [square[:, i * N : (i + 1) * N] for i in range(3)] + [jnp.zeros((5, N), F32)], axis=0
    )

    swap = copy(b["gained"], b["other"], "swap", 0, "seq", partner)
    swap.start()
    squares = []
    for k, peer in enumerate(head_peers):
        squares.append(copy(b["square"], b["squares"].at[h], "square", k, "head", peer))
        squares[-1].start()
    b["squares"][h] = b["square"][...]
    relay(4)
    arrived(high[3])
    arrived(far)
    tokens = (b["gained"], b["other"])

    def prepare(step, side):
        for way in range(2):
            chunk = (h + 2 * HEADS - 1 - step) % HEADS if way == 0 else (h + 1 + step) % HEADS
            rows = slice(way * HALF, (way + 1) * HALF)
            term = dot(tokens[side][rows, : SPLIT], b["weight_a"][chunk], 1, 1)
            term = term + dot(tokens[side][rows, SPLIT:], b["weight_b"][chunk], 1, 1)
            b["terms"][way, side] = term

    def hop(step, way, side, piece):
        at = (step, way, side, piece)
        return copy(b["send"].at[at], b["recv"].at[at], "ring", at, "head", ways[way])

    def term_of(way, side, piece):
        return b["terms"][way, side, piece * PIECE : (piece + 1) * PIECE, :]

    def summed(step, way, side, piece):
        hop(step - 1, way, side, piece).wait_recv()
        return term_of(way, side, piece) + b["recv"][step - 1, way, side, piece].astype(F32)

    places = [(side, piece, way) for side in range(2) for piece in range(2) for way in range(2)]
    prepare(0, 0)
    for side, piece, way in places:
        if (side, piece, way) == (1, 0, 0):
            swap.wait()
            prepare(0, 1)
        b["send"][0, way, side, piece] = term_of(way, side, piece).astype(BF)
        hop(0, way, side, piece).start()

    def one_step(step, carry):
        prepare(step, 0)
        prepare(step, 1)
        for side, piece, way in places:
            b["send"][step, way, side, piece] = summed(step, way, side, piece).astype(BF)
            hop(step, way, side, piece).start()
        return carry

    lax.fori_loop(1, HEADS - 1, one_step, 0)
    final = HEADS - 1
    prepare(final, 0)
    prepare(final, 1)
    homes = []
    for side, piece, way in places:
        start = way * HALF + piece * PIECE
        value = summed(final, way, side, piece)
        if side == 0:
            b["own"][start : start + PIECE, :] = value
            continue
        rows = pl.ds(start, PIECE)
        b["home"][start : start + PIECE, :] = value.astype(BF)
        at = 2 * way + piece
        homes.append(copy(b["home"].at[rows], b["home_land"].at[rows], "home", at, "seq", partner))
        homes[-1].start()
    for one in squares:
        one.wait()
    total = b["squares"][0]
    for k in range(1, HEADS):
        total = total + b["squares"][k]
    scale = columns_of(lax.rsqrt(total / DI + 1e-05))
    for one in homes:
        one.wait()
    for part in range(3):
        rows = slice(part * N, (part + 1) * N)
        factor = jnp.broadcast_to(scale[:, part : part + 1], (N, N))
        own = b["own"][rows, :]
        other = b["home_land"][rows, :].astype(F32)
        for i in range(4):
            mine = own[:, i * 64 : (i + 1) * 64]
            theirs = other[:, i * 64 : (i + 1) * 64]
            block = jnp.where(
                core == 0,
                jnp.concatenate([mine, theirs], axis=1),
                jnp.concatenate([theirs, mine], axis=1),
            )
            out_ref[rows, i * N : (i + 1) * N] = (block * factor).astype(BF)

    def drain(step, carry):
        for side, piece, way in places:
            hop(step, way, side, piece).wait_send()
        return carry

    lax.fori_loop(0, HEADS - 1, drain, 0)
    for one in sum(low + high + list(near.values()), far):
        one.wait_send()


def body(
    xbc,
    gate_z,
    dt_raw,
    dt_bias,
    a_log,
    skip_d,
    conv_weight,
    conv_bias,
    norm_gain,
    out_weight,
    starts,
):
    sems = [pltpu.SemaphoreType.DMA(shape) for shape in SEMS.values()]
    return pl.pallas_call(
        layer_kernel,
        out_shape=jax.ShapeDtypeStruct((TOK, 2 * COLS), BF),
        in_specs=[pl.BlockSpec(memory_space=pltpu.VMEM)] * 11,
        out_specs=pl.BlockSpec(memory_space=pltpu.VMEM),
        scratch_shapes=[pltpu.VMEM(*spec) for spec in SHAPES.values()] + sems + sems,
        compiler_params=pltpu.CompilerParams(collective_id=0, has_side_effects=True),
        name="layer",
    )(
        xbc, gate_z, dt_raw, dt_bias[None, :], a_log[None, :], skip_d[None, :], conv_weight,
        conv_bias, norm_gain[None, :], out_weight.T, starts,
    )


def solution(mesh):
    placed = (
        P("seq", "head"),
        P("seq", "head"),
        P("head", "seq"),
        P("head"),
        P("head"),
        P("head"),
        P(None, "head"),
        P("head"),
        P("head"),
        P("head", "seq"),
        P("seq"),
    )
    return jax.shard_map(
        body, mesh=mesh, in_specs=placed, out_specs=P("seq", "head"), check_vma=False
    )
```
